32 devices in a mesh: group: 2 (over y), cell: 8 (over z, x), day: 2 (over core).
Axes of the slice: x: 2, y: 2, z: 4, core: 2. Of those that a mesh axis runs over, the one named last changes fastest.
Arguments:
- predictors: bfloat16 [1024, 16384], P('day', 'cell'), may hold values from -180 to 180
- predictand: bfloat16 [1024, 32768], P('day', ('group', 'cell')), parts along dimension 1, may hold values from -180 to 180
- pred_map: int32 [128], P('cell'), may hold values from 0 to 127, as said below
- cell_map: int32 [256], P(('group', 'cell')), parts along dimension 0, may hold values from 0 to 127, as said below
- start_panel: bfloat16 [64, 32768], P(None, ('group', 'cell')), parts along dimension 1, may hold values from -6 to 6
Outputs:
- pred_side: float32 [64, 32768], P(None, ('group', 'cell', 'day')), parts along dimension 1
- cell_side: float32 [64, 32768], P(None, ('group', 'cell', 'day')), parts along dimension 1
The draws below stay inside these ranges and needn't reach their ends.
There are 2 independent parts, one for each index of `group`. The reference program is written for one: setup_inputs(seed, part) draws one part's arguments, and reference() takes and returns one part's arrays. A program takes and returns all parts, laid end to end along the dimension named above; an argument that names none is the same for every part. Nothing has to cross between parts.
Inputs may be any that keep to these rules, and one draw needn't show every extreme that they name: `pred_map`: aligned block s of 16 entries is a permutation of the tile numbers s * 16 to s * 16 + 15. `cell_map`: aligned block s of 16 entries is a permutation of the tile numbers s * 16 to s * 16 + 15.
All inputs are finite; a program needn't handle non-finite values.
Results may differ from the reference program's by a relative error of at most 0.02.
The reference program's roundings to bfloat16 on the way (of `pred_nat`, `cell_nat`, `scores` and `loadings`) count: a program that leaves them out, or rounds other values in their place, can miss the bound.
Values may be sent and summed in bfloat16 or wider, within the bound.
No kernel may reach another device: no remote copies, remote signals or barrier semaphores. Data moves between devices by JAX's collectives and lax.ppermute only.
A program may use at most 64 MiB of HBM per device.

```python
import jax
import jax.numpy as jnp
from jax import lax

K = 64
ITERS = 3
DAYS = 1024
PCELLS = 16384
QCELLS = 16384
PT_DEV = 16
QT_DEV = 16
PTILES = 128
QTILES = 128


def draw_field(key, rows, columns):
    first, second, third, fourth = jax.random.split(key, 4)
    spread = jax.random.uniform(first, (columns,), jnp.float32)
    mode_keys = jax.random.split(third, 4)
    load_keys = jax.random.split(fourth, 4)
    noise = jnp.clip(jax.random.normal(second, (rows, columns), jnp.float32), -6.0, 6.0)
    strengths = (1.5, 1.0, 0.7, 0.5)
    scale = jnp.power(10.0, spread)
    shared = jnp.zeros((rows, columns), jnp.float32)
    for mode_number in range(4):
        day_mode = jnp.clip(jax.random.normal(mode_keys[mode_number], (rows, 1), jnp.float32), -4.0, 4.0)
        cell_load = jax.random.uniform(load_keys[mode_number], (1, columns), jnp.float32, -1.5, 1.5)
        shared = shared + strengths[mode_number] * day_mode * cell_load
    field = (noise + shared) * scale[None, :] / 3.0
    return jnp.clip(field, -180.0, 180.0).astype(jnp.bfloat16)


def draw_tiles(key, per_block, total):
    blocks = total // per_block
    subkeys = jax.random.split(key, blocks)
    orders = jax.vmap(lambda single: jax.random.permutation(single, per_block))(subkeys)
    offsets = (jnp.arange(blocks, dtype=jnp.int32) * per_block)[:, None]
    return (orders.astype(jnp.int32) + offsets).reshape(total).astype(jnp.int32)


def draw_predictors(key, part):
    return draw_field(jax.random.fold_in(key, 11), DAYS, PCELLS)


def draw_predictand(key, part):
    return draw_field(jax.random.fold_in(key, 22), DAYS, QCELLS)


def draw_pred_map(key, part):
    return draw_tiles(jax.random.fold_in(key, 33), PT_DEV, PTILES)


def draw_cell_map(key, part):
    return draw_tiles(jax.random.fold_in(key, 44), QT_DEV, QTILES)


def block_levels(stream_key, extent, pieces, low, largest):
    def one(axis_at, blocks):
        heights = jax.random.uniform(jax.random.fold_in(jax.random.fold_in(stream_key, 6), axis_at), (blocks,), jnp.float32, low / len(pieces), largest / len(pieces))
        return jnp.repeat(jnp.exp(heights), extent[axis_at] // blocks).reshape((-1,) + (1,) * (len(extent) - axis_at - 1))

    gain = one(*pieces[0])
    for cut in pieces[1:]:
        gain = gain * one(*cut)
    return gain


def bell_draw(stream_key, extent, deviation, limit, cuts=(), kind=jnp.bfloat16):
    values = jax.random.normal(stream_key, extent, jnp.float32) * deviation
    if len(cuts) > 0:
        values = block_levels(stream_key, extent, cuts, -0.22, 0.18) * values
    return jnp.clip(values, min=-limit, max=limit).astype(kind)


def setup_inputs(seed: int = 0, part: int = 0) -> dict:
    streams_of = jax.random.split(jax.random.key(seed), 6)
    own_keys = jax.random.split(jax.random.fold_in(streams_of[5], part), 6)
    return {
        "predictors": draw_predictors(jax.random.fold_in(streams_of[5], 71), part),
        "predictand": draw_predictand(jax.random.fold_in(jax.random.fold_in(streams_of[5], part), 71), part),
        "pred_map": draw_pred_map(jax.random.fold_in(streams_of[5], 71), part),
        "cell_map": draw_cell_map(jax.random.fold_in(jax.random.fold_in(streams_of[5], part), 71), part),
        "start_panel": bell_draw(own_keys[4], (K, QCELLS), 1.0, 6.0, ((1, 8),)),
    }


def natural_order(stored, tile_map, rows, tiles):
    blocks = stored.reshape(rows, tiles, 128)
    placed = jnp.zeros_like(blocks).at[:, tile_map].set(blocks)
    return placed.reshape(rows, tiles * 128)

def orthonormal(unscaled, cell_count):
    moments = jnp.dot(unscaled.astype(jnp.float32), unscaled.T.astype(jnp.float32), precision=lax.Precision.HIGHEST, preferred_element_type=jnp.float32) / cell_count
    factor = jnp.linalg.cholesky(moments)
    return lax.linalg.triangular_solve(factor, unscaled, left_side=True, lower=True)

def reference(predictors, predictand, pred_map, cell_map, start_panel):
    pred_nat = natural_order(predictors, pred_map, DAYS, PTILES)
    cell_nat = natural_order(predictand, cell_map, DAYS, QTILES)
    current = start_panel
    contract = (((1,), (1,)), ((), ()))
    pred_side = None
    cell_side = None
    for iteration in range(ITERS):
        scores = lax.dot_general(current.astype(jnp.float32), cell_nat.astype(jnp.float32), contract, preferred_element_type=jnp.float32).astype(jnp.bfloat16)
        pred_side = orthonormal(jnp.dot(scores.astype(jnp.float32), pred_nat.astype(jnp.float32), preferred_element_type=jnp.float32), PCELLS)
        loadings = lax.dot_general(pred_side.astype(jnp.bfloat16).astype(jnp.float32), pred_nat.astype(jnp.float32), contract, preferred_element_type=jnp.float32).astype(jnp.bfloat16)
        cell_side = orthonormal(jnp.dot(loadings.astype(jnp.float32), cell_nat.astype(jnp.float32), preferred_element_type=jnp.float32), QCELLS)
        current = cell_side.astype(jnp.bfloat16)
    return (pred_side, cell_side)
```

```python
import functools

import jax
import jax.numpy as jnp
from jax import lax
from jax.experimental import pallas as pl
from jax.experimental.pallas import tpu as pltpu
from jax.sharding import PartitionSpec as P

ITERS = 3
LANES = 128
BLOCK = 256
SPLITS = 3
F32 = jnp.float32
BF16 = jnp.bfloat16
NT = (((1,), (1,)), ((), ()))
VMEM_BYTES = 50 * 1024 * 1024


def triangle(days):
    count = days // BLOCK
    return [(i, j) for i in range(count) for j in range(i, count)]


def any_spec():
    return pl.BlockSpec(memory_space=pl.ANY)


def smem_spec():
    return pl.BlockSpec(memory_space=pltpu.SMEM)


def params():
    return pltpu.CompilerParams(vmem_limit_bytes=VMEM_BYTES)


def place_kernel(place, pred_map, cell_map, pred, cell, pred_keep, pred_send, cell_keep, cell_send, sems):
    day = place[0]
    fields = ((pred_map, pred, pred_keep, pred_send), (cell_map, cell, cell_keep, cell_send))
    for f, (tile_map, stored, keep, send) in enumerate(fields):
        number = tile_map.shape[0]
        half = number // 2
        for t in range(number):
            slot = lax.rem(lax.rem(tile_map[t], number) + half * day, number)
            source = stored.at[:, pl.ds(t * LANES, LANES)]

            @pl.when(slot < half)
            def _():
                to = pl.multiple_of(slot * LANES, LANES)
                pltpu.make_async_copy(source, keep.at[:, pl.ds(to, LANES)], sems.at[f, t]).start()

            @pl.when(slot >= half)
            def _():
                to = pl.multiple_of((slot - half) * LANES, LANES)
                pltpu.make_async_copy(source, send.at[:, pl.ds(to, LANES)], sems.at[f, t]).start()

    for f, (tile_map, stored, keep, send) in enumerate(fields):
        for t in range(tile_map.shape[0]):
            part = pl.ds(0, LANES)
            pltpu.make_async_copy(stored.at[:, part], keep.at[:, part], sems.at[f, t]).wait()


def place_tiles(place, pred_map, cell_map, pred, cell):
    rows, width = pred.shape
    half = jax.ShapeDtypeStruct((rows, width // 2), pred.dtype)
    return pl.pallas_call(
        place_kernel,
        out_shape=(half,) * 4,
        in_specs=[smem_spec()] * 3 + [any_spec()] * 2,
        out_specs=(any_spec(),) * 4,
        scratch_shapes=[pltpu.SemaphoreType.DMA((2, pred_map.shape[0]))],
        compiler_params=params(),
        name="place_tiles",
    )(place, pred_map, cell_map, pred, cell)


def load_days(keep, recv, whole, day, sems):
    rows = keep.shape[0]
    first = pltpu.make_async_copy(
        keep, whole.at[pl.ds(pl.multiple_of(day * rows, rows), rows), :], sems.at[0]
    )
    second = pltpu.make_async_copy(
        recv, whole.at[pl.ds(pl.multiple_of((1 - day) * rows, rows), rows), :], sems.at[1]
    )
    return first, second


def store_block(scr, half, row, value):
    for c in range(value.shape[1] // LANES):
        height = value.shape[0]
        scr[half, pl.ds(row + c * height, height), :] = value[:, c * LANES : (c + 1) * LANES]


def flush(scr, keep, send, sems):
    one = pltpu.make_async_copy(scr.at[0], keep, sems.at[0])
    two = pltpu.make_async_copy(scr.at[1], send, sems.at[1])
    one.start()
    two.start()
    one.wait()
    two.wait()


def first_gram_kernel(blocks, place, pk, pr, ck, cr, start, keep, send, pred, cell, panel, scr, sems, outs):
    day = place[0]
    group = place[1]
    copies = load_days(pk, pr, pred, day, sems.at[0]) + load_days(ck, cr, cell, day, sems.at[1])
    width = panel.shape[1]
    begin = pl.multiple_of(day * width, width)
    copies += (pltpu.make_async_copy(start.at[:, pl.ds(begin, width)], panel, sems.at[2, 0]),)
    for copy in copies:
        copy.start()
    for copy in copies[:2]:
        copy.wait()
    share = len(blocks) // 2
    size = BLOCK * BLOCK // LANES
    per_half = (share + 1) // 2
    for k in range(share):
        i = blocks[k][0] + group * (blocks[share + k][0] - blocks[k][0])
        j = blocks[k][1] + group * (blocks[share + k][1] - blocks[k][1])
        left = pred[pl.ds(pl.multiple_of(i * BLOCK, BLOCK), BLOCK), :]
        right = pred[pl.ds(pl.multiple_of(j * BLOCK, BLOCK), BLOCK), :]
        value = lax.dot_general(left, right, NT, preferred_element_type=F32)
        half = day if k < per_half else 1 - day
        store_block(scr, half, (k % per_half) * size, value)
    for copy in copies[2:]:
        copy.wait()
    scores = lax.dot_general(panel[...], cell[...], NT, preferred_element_type=F32)
    store_block(scr, 1 - day, (share % per_half) * size, scores)
    flush(scr, keep, send, outs)


def second_gram_kernel(blocks, place, ck, cr, keep, send, cell, scr, sems, outs):
    day = place[0]
    copies = load_days(ck, cr, cell, day, sems)
    for copy in copies:
        copy.start()
    for copy in copies:
        copy.wait()
    size = BLOCK * BLOCK // LANES
    per_half = len(blocks) // 2
    for k, (i, j) in enumerate(blocks):
        value = lax.dot_general(
            cell[i * BLOCK : (i + 1) * BLOCK, :],
            cell[j * BLOCK : (j + 1) * BLOCK, :],
            NT,
            preferred_element_type=F32,
        )
        half = day if k < per_half else 1 - day
        store_block(scr, half, (k % per_half) * size, value)
    flush(scr, keep, send, outs)


def first_gram(place, pk, pr, ck, cr, start):
    days, width = 2 * pk.shape[0], pk.shape[1]
    blocks = triangle(days)
    rows = (len(blocks) // 2 + 1) // 2 * (BLOCK * BLOCK // LANES)
    out = jax.ShapeDtypeStruct((rows, LANES), F32)
    return pl.pallas_call(
        functools.partial(first_gram_kernel, blocks),
        out_shape=(out, out),
        in_specs=[smem_spec()] + [any_spec()] * 5,
        out_specs=(any_spec(), any_spec()),
        scratch_shapes=[
            pltpu.VMEM((days, width), BF16),
            pltpu.VMEM((days, width), BF16),
            pltpu.VMEM((start.shape[0], width), BF16),
            pltpu.VMEM((2, rows, LANES), F32),
            pltpu.SemaphoreType.DMA((3, 2)),
            pltpu.SemaphoreType.DMA((2,)),
        ],
        compiler_params=params(),
        name="first_gram",
    )(place, pk, pr, ck, cr, start)


def second_gram(place, ck, cr):
    days, width = 2 * ck.shape[0], ck.shape[1]
    blocks = triangle(days)
    rows = len(blocks) // 2 * (BLOCK * BLOCK // LANES)
    out = jax.ShapeDtypeStruct((rows, LANES), F32)
    return pl.pallas_call(
        functools.partial(second_gram_kernel, blocks),
        out_shape=(out, out),
        in_specs=[smem_spec()] + [any_spec()] * 2,
        out_specs=(any_spec(), any_spec()),
        scratch_shapes=[
            pltpu.VMEM((days, width), BF16),
            pltpu.VMEM((2, rows, LANES), F32),
            pltpu.SemaphoreType.DMA((2,)),
            pltpu.SemaphoreType.DMA((2,)),
        ],
        compiler_params=params(),
        name="second_gram",
    )(place, ck, cr)


def bit_orders(bits):
    plain = list(range(bits))
    swapped = plain[:]
    if bits > 2:
        swapped[0], swapped[1] = 1, 0
    return plain, swapped


def cell_exchange(value, orders, stage, cells):
    pairs = []
    for c in range(cells):
        for d in range(2):
            pairs.append((2 * c + d, 2 * (c ^ (1 << orders[d][stage])) + d))
    return lax.ppermute(value, ("cell", "day"), pairs)


def other_core(value):
    return lax.ppermute(value, "day", [(0, 1), (1, 0)])


def sum_over_cells(keep, send):
    cells = lax.axis_size("cell")
    bits = cells.bit_length() - 1
    orders = bit_orders(bits)
    cell = lax.axis_index("cell")
    day = lax.axis_index("day")
    recv = other_core(send)
    mine = keep
    for stage in range(bits - 1):
        bit = jnp.where(day == 0, orders[0][stage], orders[1][stage])
        own = (cell >> bit) & 1
        half = mine.shape[0] // 2
        away = lax.dynamic_slice_in_dim(mine, (1 - own) * half, half, 0)
        away = away + lax.dynamic_slice_in_dim(recv, (1 - own) * half, half, 0)
        home = lax.dynamic_slice_in_dim(mine, own * half, half, 0)
        home = home + lax.dynamic_slice_in_dim(recv, own * half, half, 0)
        recv = cell_exchange(away, orders, stage, cells)
        mine = home
    part = mine + recv
    part = part + cell_exchange(part, orders, bits - 1, cells)
    for stage in reversed(range(bits - 1)):
        part = jnp.concatenate([part, cell_exchange(part, orders, stage, cells)], axis=0)
    return part


def placed_copies(source, target, half, bits, order, cell, sem):
    pieces = 1 << (bits - 1)
    rows = source.shape[0] // pieces
    copies = []
    for p in range(pieces):
        to = 0
        for stage in range(bits - 1):
            digit = (p >> (bits - 2 - stage)) & 1
            own = (cell >> order[stage]) & 1
            to = 2 * to + (own ^ digit)
        begin = pl.multiple_of(to * rows, 8)
        copies.append(
            pltpu.make_async_copy(
                source.at[pl.ds(p * rows, rows), :], target.at[half, pl.ds(begin, rows), :], sem.at[p]
            )
        )
    return copies


def load_block(packed, half, row, height, width):
    tiles = [packed[half, pl.ds(row + c * height, height), :] for c in range(width // LANES)]
    return jnp.concatenate(tiles, axis=1)


def split3(value):
    first = value.astype(BF16)
    rest = value - first.astype(F32)
    second = rest.astype(BF16)
    third = (rest - second.astype(F32)).astype(BF16)
    return first, second, third


def assemble(packed, half, row, i, j, gram):
    value = load_block(packed, half, row, BLOCK, BLOCK)
    rows, cols = pl.ds(i * BLOCK, BLOCK), pl.ds(j * BLOCK, BLOCK)
    for s, piece in enumerate(split3(value)):
        gram[s, rows, cols] = piece
    if i != j:
        for s, piece in enumerate(split3(value.T)):
            gram[s, cols, rows] = piece


def exact_dot(left, right):
    return jnp.dot(left, right, precision=lax.Precision.HIGHEST, preferred_element_type=F32)


def inverse_factor(moments):
    k_rows = moments.shape[0]
    row_ids = lax.broadcasted_iota(jnp.int32, (k_rows, k_rows), 0)
    col_ids = lax.broadcasted_iota(jnp.int32, (k_rows, k_rows), 1)
    work = jnp.concatenate([moments, (row_ids == col_ids).astype(F32)], axis=1)
    below = lax.broadcasted_iota(jnp.int32, (k_rows, 1), 0)
    scale = jnp.ones((k_rows, 1), F32)
    for k in range(k_rows):
        row = work[k : k + 1, :]
        column = work[:, k : k + 1]
        pivot = work[k : k + 1, k : k + 1]
        factor = jnp.where(below > k, column / pivot, 0.0)
        scale = jnp.where(below == k, 1.0 / jnp.sqrt(pivot), scale)
        work = work - factor * row
    return work[:, k_rows:] * scale


def half_step(scores, gram, cells):
    value = jnp.dot(scores, gram[0], preferred_element_type=F32)
    for s in range(1, SPLITS):
        value = value + jnp.dot(scores, gram[s], preferred_element_type=F32)
    moments = sum(
        lax.dot_general(piece, scores, NT, preferred_element_type=F32) for piece in split3(value)
    )
    inverse = inverse_factor(moments / cells)
    return inverse, exact_dot(inverse, value).astype(BF16)


def chain_kernel(
    blocks, bits, orders, counts, place,
    a_own, a_twin, y_own, y_twin, b_own, b_twin, pk, pr, ck, cr,
    pred_out, cell_out,
    alpha, other, beta, pred, cell, pred_gram, cell_gram, sems, data_sems,
):
    day, group, index = place[0], place[1], place[2]
    data = load_days(pk, pr, pred, day, data_sems.at[0]) + load_days(ck, cr, cell, day, data_sems.at[1])
    for copy in data:
        copy.start()

    def gather(core):
        own, twin = orders[core], orders[1 - core]
        copies = []
        for n, (source, target, half, order) in enumerate(
            (
                (a_own, alpha, core, own),
                (a_twin, alpha, 1 - core, twin),
                (y_own, other, core, own),
                (y_twin, other, 1 - core, twin),
                (b_own, beta, core, own),
                (b_twin, beta, 1 - core, twin),
            )
        ):
            copies += placed_copies(source, target, half, bits, order, index, sems.at[n])
        for copy in copies:
            copy.start()
        for copy in copies:
            copy.wait()

    @pl.when(day == 0)
    def _():
        gather(0)

    @pl.when(day == 1)
    def _():
        gather(1)

    size = BLOCK * BLOCK // LANES
    share = len(blocks) // 2
    per_half = (share + 1) // 2

    def assemble_pred(mine, theirs):
        for g, packed in enumerate((mine, theirs)):
            for k in range(share):
                i, j = blocks[g * share + k]
                assemble(packed, k // per_half, (k % per_half) * size, i, j, pred_gram)

    @pl.when(group == 0)
    def _():
        assemble_pred(alpha, other)

    @pl.when(group == 1)
    def _():
        assemble_pred(other, alpha)

    for k, (i, j) in enumerate(blocks):
        assemble(beta, k // share, (k % share) * size, i, j, cell_gram)

    days = pred.shape[0]
    height = pred_out.shape[0]
    scores = load_block(alpha, 1, (share % per_half) * size, height, days).astype(BF16)
    pred_inverse = cell_inverse = pred_scores = loadings = None
    for _ in range(ITERS):
        pred_scores = scores
        pred_inverse, loadings = half_step(scores, pred_gram, counts[0])
        cell_inverse, scores = half_step(loadings, cell_gram, counts[1])
    for copy in data:
        copy.wait()
    raw = jnp.dot(pred_scores, pred[...], preferred_element_type=F32)
    pred_out[...] = exact_dot(pred_inverse, raw)
    raw = jnp.dot(loadings, cell[...], preferred_element_type=F32)
    cell_out[...] = exact_dot(cell_inverse, raw)


def local(predictors, predictand, pred_map, cell_map, start_panel):
    cells = lax.axis_size("cell")
    bits = cells.bit_length() - 1
    orders = bit_orders(bits)
    days = predictors.shape[0] * 2
    width = predictors.shape[1] // 2
    height = start_panel.shape[0]
    counts = (float(predictors.shape[1] * cells), float(predictand.shape[1] * cells))
    blocks = triangle(days)
    place = jnp.stack([lax.axis_index("day"), lax.axis_index("group"), lax.axis_index("cell")])
    place = place.astype(jnp.int32)

    pk, ps, ck, cs = place_tiles(place, pred_map, cell_map, predictors, predictand)
    pr = other_core(ps)
    cr = other_core(cs)
    a_keep, a_send = first_gram(place, pk, pr, ck, cr, start_panel)
    b_keep, b_send = second_gram(place, ck, cr)
    a_own = sum_over_cells(a_keep, a_send)
    y_own = lax.ppermute(a_own, "group", [(0, 1), (1, 0)])
    b_own = sum_over_cells(b_keep, b_send)
    a_twin = other_core(a_own)
    y_twin = other_core(y_own)
    b_twin = other_core(b_own)

    out = jax.ShapeDtypeStruct((height, width), F32)
    pieces = 1 << (bits - 1)
    return pl.pallas_call(
        functools.partial(chain_kernel, blocks, bits, orders, counts),
        out_shape=(out, out),
        in_specs=[smem_spec()] + [any_spec()] * 10,
        scratch_shapes=[
            pltpu.VMEM((2,) + a_own.shape, F32),
            pltpu.VMEM((2,) + a_own.shape, F32),
            pltpu.VMEM((2,) + b_own.shape, F32),
            pltpu.VMEM((days, width), BF16),
            pltpu.VMEM((days, width), BF16),
            pltpu.VMEM((SPLITS, days, days), BF16),
            pltpu.VMEM((SPLITS, days, days), BF16),
            pltpu.SemaphoreType.DMA((6, pieces)),
            pltpu.SemaphoreType.DMA((2, 2)),
        ],
        compiler_params=params(),
        name="chain",
    )(place, a_own, a_twin, y_own, y_twin, b_own, b_twin, pk, pr, ck, cr)


def solution(mesh):
    in_specs = (
        P("day", "cell"),
        P("day", ("group", "cell")),
        P("cell"),
        P(("group", "cell")),
        P(None, ("group", "cell")),
    )
    out_specs = (P(None, ("group", "cell", "day")), P(None, ("group", "cell", "day")))
    return jax.shard_map(local, mesh=mesh, in_specs=in_specs, out_specs=out_specs, check_vma=False)
```

```python
import functools

import jax
import jax.numpy as jnp
from jax import lax
from jax.experimental import pallas as pl
from jax.experimental.pallas import tpu as pltpu
from jax.sharding import PartitionSpec as P

ITERS = 3
LANES = 128
BLOCK = 256
SPLITS = 3
F32 = jnp.float32
BF16 = jnp.bfloat16
NT = (((1,), (1,)), ((), ()))
VMEM_BYTES = 50 * 1024 * 1024


def triangle(days):
    count = days // BLOCK
    return [(i, j) for i in range(count) for j in range(i, count)]


def any_spec():
    return pl.BlockSpec(memory_space=pl.ANY)


def smem_spec():
    return pl.BlockSpec(memory_space=pltpu.SMEM)


def params():
    return pltpu.CompilerParams(vmem_limit_bytes=VMEM_BYTES)


def place_kernel(
    place, pred_map, cell_map, pred, cell, pred_keep, pred_send, cell_keep, cell_send, pred_buf, cell_buf, sems, outs
):
    day = place[0]
    fields = ((pred_map, pred, pred_buf, pred_keep, pred_send), (cell_map, cell, cell_buf, cell_keep, cell_send))
    loads = []
    for f, (tile_map, stored, buf, keep, send) in enumerate(fields):
        number = tile_map.shape[0]
        half = number // 2
        for t in range(number):
            slot = lax.rem(lax.rem(tile_map[t], number) + half * day, number)
            to = pl.multiple_of(lax.rem(slot, half) * LANES, LANES)
            loads.append(
                pltpu.make_async_copy(
                    stored.at[:, pl.ds(t * LANES, LANES)],
                    buf.at[lax.div(slot, half), :, pl.ds(to, LANES)],
                    sems.at[f, t],
                )
            )
    for copy in loads:
        copy.start()
    stores = []
    number = pred_map.shape[0]
    for f, (tile_map, stored, buf, keep, send) in enumerate(fields):
        for copy in loads[f * number : (f + 1) * number]:
            copy.wait()
        for n, target in ((1, send), (0, keep)):
            copy = pltpu.make_async_copy(buf.at[n], target, outs.at[f, n])
            copy.start()
            stores.append(copy)
    for copy in stores:
        copy.wait()


def place_tiles(place, pred_map, cell_map, pred, cell):
    rows, width = pred.shape
    half = jax.ShapeDtypeStruct((rows, width // 2), pred.dtype)
    return pl.pallas_call(
        place_kernel,
        out_shape=(half,) * 4,
        in_specs=[smem_spec()] * 3 + [any_spec()] * 2,
        out_specs=(any_spec(),) * 4,
        scratch_shapes=[
            pltpu.VMEM((2, rows, width // 2), pred.dtype),
            pltpu.VMEM((2, rows, width // 2), pred.dtype),
            pltpu.SemaphoreType.DMA((2, pred_map.shape[0])),
            pltpu.SemaphoreType.DMA((2, 2)),
        ],
        compiler_params=params(),
        name="place_tiles",
    )(place, pred_map, cell_map, pred, cell)


def load_days(keep, recv, whole, day, sems):
    rows = keep.shape[0]
    first = pltpu.make_async_copy(
        keep, whole.at[pl.ds(pl.multiple_of(day * rows, rows), rows), :], sems.at[0]
    )
    second = pltpu.make_async_copy(
        recv, whole.at[pl.ds(pl.multiple_of((1 - day) * rows, rows), rows), :], sems.at[1]
    )
    return first, second


def store_block(scr, half, row, value):
    for c in range(value.shape[1] // LANES):
        height = value.shape[0]
        scr[half, pl.ds(row + c * height, height), :] = value[:, c * LANES : (c + 1) * LANES]


def flush(scr, keep, send, sems):
    one = pltpu.make_async_copy(scr.at[0], keep, sems.at[0])
    two = pltpu.make_async_copy(scr.at[1], send, sems.at[1])
    one.start()
    two.start()
    one.wait()
    two.wait()


def first_gram_kernel(blocks, place, pk, pr, ck, cr, start, keep, send, pred, cell, panel, scr, sems, outs):
    day = place[0]
    group = place[1]
    copies = load_days(pk, pr, pred, day, sems.at[0]) + load_days(ck, cr, cell, day, sems.at[1])
    width = panel.shape[1]
    begin = pl.multiple_of(day * width, width)
    copies += (pltpu.make_async_copy(start.at[:, pl.ds(begin, width)], panel, sems.at[2, 0]),)
    for copy in copies:
        copy.start()
    for copy in copies[:2]:
        copy.wait()
    share = len(blocks) // 2
    size = BLOCK * BLOCK // LANES
    per_half = (share + 1) // 2
    for k in range(share):
        i = blocks[k][0] + group * (blocks[share + k][0] - blocks[k][0])
        j = blocks[k][1] + group * (blocks[share + k][1] - blocks[k][1])
        left = pred[pl.ds(pl.multiple_of(i * BLOCK, BLOCK), BLOCK), :]
        right = pred[pl.ds(pl.multiple_of(j * BLOCK, BLOCK), BLOCK), :]
        value = lax.dot_general(left, right, NT, preferred_element_type=F32)
        half = day if k < per_half else 1 - day
        store_block(scr, half, (k % per_half) * size, value)
    for copy in copies[2:]:
        copy.wait()
    scores = lax.dot_general(panel[...], cell[...], NT, preferred_element_type=F32)
    store_block(scr, 1 - day, (share % per_half) * size, scores)
    flush(scr, keep, send, outs)


def second_gram_kernel(blocks, place, ck, cr, after, keep, send, cell, scr, sems, outs):
    day = place[0]
    copies = load_days(ck, cr, cell, day, sems)
    for copy in copies:
        copy.start()
    for copy in copies:
        copy.wait()
    size = BLOCK * BLOCK // LANES
    per_half = len(blocks) // 2
    for k, (i, j) in enumerate(blocks):
        value = lax.dot_general(
            cell[i * BLOCK : (i + 1) * BLOCK, :],
            cell[j * BLOCK : (j + 1) * BLOCK, :],
            NT,
            preferred_element_type=F32,
        )
        half = day if k < per_half else 1 - day
        store_block(scr, half, (k % per_half) * size, value)
    flush(scr, keep, send, outs)


def first_gram(place, pk, pr, ck, cr, start):
    days, width = 2 * pk.shape[0], pk.shape[1]
    blocks = triangle(days)
    rows = (len(blocks) // 2 + 1) // 2 * (BLOCK * BLOCK // LANES)
    out = jax.ShapeDtypeStruct((rows, LANES), F32)
    return pl.pallas_call(
        functools.partial(first_gram_kernel, blocks),
        out_shape=(out, out),
        in_specs=[smem_spec()] + [any_spec()] * 5,
        out_specs=(any_spec(), any_spec()),
        scratch_shapes=[
            pltpu.VMEM((days, width), BF16),
            pltpu.VMEM((days, width), BF16),
            pltpu.VMEM((start.shape[0], width), BF16),
            pltpu.VMEM((2, rows, LANES), F32),
            pltpu.SemaphoreType.DMA((3, 2)),
            pltpu.SemaphoreType.DMA((2,)),
        ],
        compiler_params=params(),
        name="first_gram",
    )(place, pk, pr, ck, cr, start)


def second_gram(place, ck, cr, after):
    days, width = 2 * ck.shape[0], ck.shape[1]
    blocks = triangle(days)
    rows = len(blocks) // 2 * (BLOCK * BLOCK // LANES)
    out = jax.ShapeDtypeStruct((rows, LANES), F32)
    return pl.pallas_call(
        functools.partial(second_gram_kernel, blocks),
        out_shape=(out, out),
        in_specs=[smem_spec()] + [any_spec()] * 3,
        out_specs=(any_spec(), any_spec()),
        scratch_shapes=[
            pltpu.VMEM((days, width), BF16),
            pltpu.VMEM((2, rows, LANES), F32),
            pltpu.SemaphoreType.DMA((2,)),
            pltpu.SemaphoreType.DMA((2,)),
        ],
        compiler_params=params(),
        name="second_gram",
    )(place, ck, cr, after)


def bit_orders(bits):
    plain = list(range(bits))
    swapped = plain[:]
    if bits > 2:
        swapped[0], swapped[1] = 1, 0
    return plain, swapped


def cell_exchange(value, orders, stage, cells):
    pairs = []
    for c in range(cells):
        for d in range(2):
            pairs.append((2 * c + d, 2 * (c ^ (1 << orders[d][stage])) + d))
    return lax.ppermute(value, ("cell", "day"), pairs)


def other_core(value):
    return lax.ppermute(value, "day", [(0, 1), (1, 0)])


def sum_over_cells(keep, send):
    cells = lax.axis_size("cell")
    bits = cells.bit_length() - 1
    orders = bit_orders(bits)
    cell = lax.axis_index("cell")
    day = lax.axis_index("day")
    recv = other_core(send)
    mine = keep
    for stage in range(bits - 1):
        bit = jnp.where(day == 0, orders[0][stage], orders[1][stage])
        own = (cell >> bit) & 1
        half = mine.shape[0] // 2
        away = lax.dynamic_slice_in_dim(mine, (1 - own) * half, half, 0)
        away = away + lax.dynamic_slice_in_dim(recv, (1 - own) * half, half, 0)
        home = lax.dynamic_slice_in_dim(mine, own * half, half, 0)
        home = home + lax.dynamic_slice_in_dim(recv, own * half, half, 0)
        recv = cell_exchange(away, orders, stage, cells)
        mine = home
    part = mine + recv
    part = part + cell_exchange(part, orders, bits - 1, cells)
    for stage in reversed(range(bits - 1)):
        part = jnp.concatenate([part, cell_exchange(part, orders, stage, cells)], axis=0)
    return part


def placed_copies(source, target, half, bits, order, cell, sem):
    pieces = 1 << (bits - 1)
    rows = source.shape[0] // pieces
    copies = []
    for p in range(pieces):
        to = 0
        for stage in range(bits - 1):
            digit = (p >> (bits - 2 - stage)) & 1
            own = (cell >> order[stage]) & 1
            to = 2 * to + (own ^ digit)
        begin = pl.multiple_of(to * rows, 8)
        copies.append(
            pltpu.make_async_copy(
                source.at[pl.ds(p * rows, rows), :], target.at[half, pl.ds(begin, rows), :], sem.at[p]
            )
        )
    return copies


def load_block(packed, half, row, height, width):
    tiles = [packed[half, pl.ds(row + c * height, height), :] for c in range(width // LANES)]
    return jnp.concatenate(tiles, axis=1)


def split3(value):
    first = value.astype(BF16)
    rest = value - first.astype(F32)
    second = rest.astype(BF16)
    third = (rest - second.astype(F32)).astype(BF16)
    return first, second, third


def assemble(packed, half, row, i, j, gram):
    value = load_block(packed, half, row, BLOCK, BLOCK)
    rows, cols = pl.ds(i * BLOCK, BLOCK), pl.ds(j * BLOCK, BLOCK)
    for s, piece in enumerate(split3(value)):
        gram[s, rows, cols] = piece
    if i != j:
        for s, piece in enumerate(split3(value.T)):
            gram[s, cols, rows] = piece


def exact_dot(left, right):
    return jnp.dot(left, right, precision=lax.Precision.HIGHEST, preferred_element_type=F32)


def inverse_factor(moments):
    k_rows = moments.shape[0]
    row_ids = lax.broadcasted_iota(jnp.int32, (k_rows, k_rows), 0)
    col_ids = lax.broadcasted_iota(jnp.int32, (k_rows, k_rows), 1)
    work = jnp.concatenate([moments, (row_ids == col_ids).astype(F32)], axis=1)
    below = lax.broadcasted_iota(jnp.int32, (k_rows, 1), 0)
    scale = jnp.ones((k_rows, 1), F32)
    for k in range(k_rows):
        row = work[k : k + 1, :]
        column = work[:, k : k + 1]
        pivot = work[k : k + 1, k : k + 1]
        factor = jnp.where(below > k, column / pivot, 0.0)
        scale = jnp.where(below == k, 1.0 / jnp.sqrt(pivot), scale)
        work = work - factor * row
    return work[:, k_rows:] * scale


def half_step(scores, gram, cells):
    value = jnp.dot(scores, gram[0], preferred_element_type=F32)
    for s in range(1, SPLITS):
        value = value + jnp.dot(scores, gram[s], preferred_element_type=F32)
    moments = sum(
        lax.dot_general(piece, scores, NT, preferred_element_type=F32) for piece in split3(value)
    )
    inverse = inverse_factor(moments / cells)
    return inverse, exact_dot(inverse, value).astype(BF16)


def chain_kernel(
    blocks, bits, orders, counts, place,
    a_own, a_twin, y_own, y_twin, b_own, b_twin, pk, pr, ck, cr,
    pred_out, cell_out,
    alpha, other, beta, pred, cell, pred_gram, cell_gram, sems, data_sems,
):
    day, group, index = place[0], place[1], place[2]
    data = load_days(pk, pr, pred, day, data_sems.at[0]) + load_days(ck, cr, cell, day, data_sems.at[1])
    for copy in data:
        copy.start()

    def gather(core):
        own, twin = orders[core], orders[1 - core]
        copies = []
        for n, (source, target, half, order) in enumerate(
            (
                (a_own, alpha, core, own),
                (a_twin, alpha, 1 - core, twin),
                (y_own, other, core, own),
                (y_twin, other, 1 - core, twin),
                (b_own, beta, core, own),
                (b_twin, beta, 1 - core, twin),
            )
        ):
            copies += placed_copies(source, target, half, bits, order, index, sems.at[n])
        for copy in copies:
            copy.start()
        for copy in copies:
            copy.wait()

    @pl.when(day == 0)
    def _():
        gather(0)

    @pl.when(day == 1)
    def _():
        gather(1)

    size = BLOCK * BLOCK // LANES
    share = len(blocks) // 2
    per_half = (share + 1) // 2

    def assemble_pred(mine, theirs):
        for g, packed in enumerate((mine, theirs)):
            for k in range(share):
                i, j = blocks[g * share + k]
                assemble(packed, k // per_half, (k % per_half) * size, i, j, pred_gram)

    @pl.when(group == 0)
    def _():
        assemble_pred(alpha, other)

    @pl.when(group == 1)
    def _():
        assemble_pred(other, alpha)

    for k, (i, j) in enumerate(blocks):
        assemble(beta, k // share, (k % share) * size, i, j, cell_gram)

    days = pred.shape[0]
    height = pred_out.shape[0]
    scores = load_block(alpha, 1, (share % per_half) * size, height, days).astype(BF16)
    pred_inverse = cell_inverse = pred_scores = loadings = None
    for _ in range(ITERS):
        pred_scores = scores
        pred_inverse, loadings = half_step(scores, pred_gram, counts[0])
        cell_inverse, scores = half_step(loadings, cell_gram, counts[1])
    for copy in data:
        copy.wait()
    raw = jnp.dot(pred_scores, pred[...], preferred_element_type=F32)
    pred_out[...] = exact_dot(pred_inverse, raw)
    raw = jnp.dot(loadings, cell[...], preferred_element_type=F32)
    cell_out[...] = exact_dot(cell_inverse, raw)


def local(predictors, predictand, pred_map, cell_map, start_panel):
    cells = lax.axis_size("cell")
    bits = cells.bit_length() - 1
    orders = bit_orders(bits)
    days = predictors.shape[0] * 2
    width = predictors.shape[1] // 2
    height = start_panel.shape[0]
    counts = (float(predictors.shape[1] * cells), float(predictand.shape[1] * cells))
    blocks = triangle(days)
    place = jnp.stack([lax.axis_index("day"), lax.axis_index("group"), lax.axis_index("cell")])
    place = place.astype(jnp.int32)

    pk, ps, ck, cs = place_tiles(place, pred_map, cell_map, predictors, predictand)
    pr = other_core(ps)
    cr = other_core(cs)
    a_keep, a_send = first_gram(place, pk, pr, ck, cr, start_panel)
    b_keep, b_send = second_gram(place, ck, cr, a_keep)
    a_own = sum_over_cells(a_keep, a_send)
    y_own = lax.ppermute(a_own, "group", [(0, 1), (1, 0)])
    b_own = sum_over_cells(b_keep, b_send)
    a_twin = other_core(a_own)
    y_twin = other_core(y_own)
    b_twin = other_core(b_own)

    out = jax.ShapeDtypeStruct((height, width), F32)
    pieces = 1 << (bits - 1)
    return pl.pallas_call(
        functools.partial(chain_kernel, blocks, bits, orders, counts),
        out_shape=(out, out),
        in_specs=[smem_spec()] + [any_spec()] * 10,
        scratch_shapes=[
            pltpu.VMEM((2,) + a_own.shape, F32),
            pltpu.VMEM((2,) + a_own.shape, F32),
            pltpu.VMEM((2,) + b_own.shape, F32),
            pltpu.VMEM((days, width), BF16),
            pltpu.VMEM((days, width), BF16),
            pltpu.VMEM((SPLITS, days, days), BF16),
            pltpu.VMEM((SPLITS, days, days), BF16),
            pltpu.SemaphoreType.DMA((6, pieces)),
            pltpu.SemaphoreType.DMA((2, 2)),
        ],
        compiler_params=params(),
        name="chain",
    )(place, a_own, a_twin, y_own, y_twin, b_own, b_twin, pk, pr, ck, cr)


def solution(mesh):
    in_specs = (
        P("day", "cell"),
        P("day", ("group", "cell")),
        P("cell"),
        P(("group", "cell")),
        P(None, ("group", "cell")),
    )
    out_specs = (P(None, ("group", "cell", "day")), P(None, ("group", "cell", "day")))
    return jax.shard_map(local, mesh=mesh, in_specs=in_specs, out_specs=out_specs, check_vma=False)
```

```python
import functools

import jax
import jax.numpy as jnp
from jax import lax
from jax.experimental import pallas as pl
from jax.experimental.pallas import tpu as pltpu
from jax.sharding import PartitionSpec as P

ITERS = 3
LANES = 128
BLOCK = 256
SPLITS = 3
SUB = 8
F32 = jnp.float32
BF16 = jnp.bfloat16
NT = (((1,), (1,)), ((), ()))
VMEM_BYTES = 50 * 1024 * 1024


def triangle(days):
    count = days // BLOCK
    return [(i, j) for i in range(count) for j in range(i, count)]


def any_spec():
    return pl.BlockSpec(memory_space=pl.ANY)


def smem_spec():
    return pl.BlockSpec(memory_space=pltpu.SMEM)


def params():
    return pltpu.CompilerParams(vmem_limit_bytes=VMEM_BYTES)


def place_kernel(
    place, pred_map, cell_map, pred, cell, pred_keep, pred_send, cell_keep, cell_send, pred_buf, cell_buf, sems, outs
):
    day = place[0]
    fields = ((pred_map, pred, pred_buf, pred_keep, pred_send), (cell_map, cell, cell_buf, cell_keep, cell_send))
    loads = []
    for f, (tile_map, stored, buf, keep, send) in enumerate(fields):
        number = tile_map.shape[0]
        half = number // 2
        for t in range(number):
            slot = lax.rem(lax.rem(tile_map[t], number) + half * day, number)
            to = pl.multiple_of(lax.rem(slot, half) * LANES, LANES)
            loads.append(
                pltpu.make_async_copy(
                    stored.at[:, pl.ds(t * LANES, LANES)],
                    buf.at[lax.div(slot, half), :, pl.ds(to, LANES)],
                    sems.at[f, t],
                )
            )
    for copy in loads:
        copy.start()
    stores = []
    number = pred_map.shape[0]
    for f, (tile_map, stored, buf, keep, send) in enumerate(fields):
        for copy in loads[f * number : (f + 1) * number]:
            copy.wait()
        for n, target in ((1, send), (0, keep)):
            copy = pltpu.make_async_copy(buf.at[n], target, outs.at[f, n])
            copy.start()
            stores.append(copy)
    for copy in stores:
        copy.wait()


def place_tiles(place, pred_map, cell_map, pred, cell):
    rows, width = pred.shape
    half = jax.ShapeDtypeStruct((rows, width // 2), pred.dtype)
    return pl.pallas_call(
        place_kernel,
        out_shape=(half,) * 4,
        in_specs=[smem_spec()] * 3 + [any_spec()] * 2,
        out_specs=(any_spec(),) * 4,
        scratch_shapes=[
            pltpu.VMEM((2, rows, width // 2), pred.dtype),
            pltpu.VMEM((2, rows, width // 2), pred.dtype),
            pltpu.SemaphoreType.DMA((2, pred_map.shape[0])),
            pltpu.SemaphoreType.DMA((2, 2)),
        ],
        compiler_params=params(),
        name="place_tiles",
    )(place, pred_map, cell_map, pred, cell)


def load_days(keep, recv, whole, day, sems):
    rows = keep.shape[0]
    first = pltpu.make_async_copy(
        keep, whole.at[pl.ds(pl.multiple_of(day * rows, rows), rows), :], sems.at[0]
    )
    second = pltpu.make_async_copy(
        recv, whole.at[pl.ds(pl.multiple_of((1 - day) * rows, rows), rows), :], sems.at[1]
    )
    return first, second


def store_block(scr, half, row, value):
    for c in range(value.shape[1] // LANES):
        height = value.shape[0]
        scr[half, pl.ds(row + c * height, height), :] = value[:, c * LANES : (c + 1) * LANES]


def flush(scr, keep, send, sems):
    one = pltpu.make_async_copy(scr.at[0], keep, sems.at[0])
    two = pltpu.make_async_copy(scr.at[1], send, sems.at[1])
    one.start()
    two.start()
    one.wait()
    two.wait()


def first_gram_kernel(blocks, place, pk, pr, ck, cr, start, keep, send, pred, cell, panel, scr, sems, outs):
    day = place[0]
    group = place[1]
    copies = load_days(pk, pr, pred, day, sems.at[0]) + load_days(ck, cr, cell, day, sems.at[1])
    width = panel.shape[1]
    begin = pl.multiple_of(day * width, width)
    copies += (pltpu.make_async_copy(start.at[:, pl.ds(begin, width)], panel, sems.at[2, 0]),)
    for copy in copies:
        copy.start()
    for copy in copies[:2]:
        copy.wait()
    share = len(blocks) // 2
    size = BLOCK * BLOCK // LANES
    per_half = (share + 1) // 2
    for k in range(share):
        i = blocks[k][0] + group * (blocks[share + k][0] - blocks[k][0])
        j = blocks[k][1] + group * (blocks[share + k][1] - blocks[k][1])
        left = pred[pl.ds(pl.multiple_of(i * BLOCK, BLOCK), BLOCK), :]
        right = pred[pl.ds(pl.multiple_of(j * BLOCK, BLOCK), BLOCK), :]
        value = lax.dot_general(left, right, NT, preferred_element_type=F32)
        half = day if k < per_half else 1 - day
        store_block(scr, half, (k % per_half) * size, value)
    for copy in copies[2:]:
        copy.wait()
    scores = lax.dot_general(panel[...], cell[...], NT, preferred_element_type=F32)
    store_block(scr, 1 - day, (share % per_half) * size, scores)
    flush(scr, keep, send, outs)


def second_gram_kernel(blocks, place, ck, cr, after, keep, send, cell, scr, sems, outs):
    day = place[0]
    copies = load_days(ck, cr, cell, day, sems)
    for copy in copies:
        copy.start()
    for copy in copies:
        copy.wait()
    size = BLOCK * BLOCK // LANES
    per_half = len(blocks) // 2
    for k, (i, j) in enumerate(blocks):
        value = lax.dot_general(
            cell[i * BLOCK : (i + 1) * BLOCK, :],
            cell[j * BLOCK : (j + 1) * BLOCK, :],
            NT,
            preferred_element_type=F32,
        )
        half = day if k < per_half else 1 - day
        store_block(scr, half, (k % per_half) * size, value)
    flush(scr, keep, send, outs)


def first_gram(place, pk, pr, ck, cr, start):
    days, width = 2 * pk.shape[0], pk.shape[1]
    blocks = triangle(days)
    rows = (len(blocks) // 2 + 1) // 2 * (BLOCK * BLOCK // LANES)
    out = jax.ShapeDtypeStruct((rows, LANES), F32)
    return pl.pallas_call(
        functools.partial(first_gram_kernel, blocks),
        out_shape=(out, out),
        in_specs=[smem_spec()] + [any_spec()] * 5,
        out_specs=(any_spec(), any_spec()),
        scratch_shapes=[
            pltpu.VMEM((days, width), BF16),
            pltpu.VMEM((days, width), BF16),
            pltpu.VMEM((start.shape[0], width), BF16),
            pltpu.VMEM((2, rows, LANES), F32),
            pltpu.SemaphoreType.DMA((3, 2)),
            pltpu.SemaphoreType.DMA((2,)),
        ],
        compiler_params=params(),
        name="first_gram",
    )(place, pk, pr, ck, cr, start)


def second_gram(place, ck, cr, after):
    days, width = 2 * ck.shape[0], ck.shape[1]
    blocks = triangle(days)
    rows = len(blocks) // 2 * (BLOCK * BLOCK // LANES)
    out = jax.ShapeDtypeStruct((rows, LANES), F32)
    return pl.pallas_call(
        functools.partial(second_gram_kernel, blocks),
        out_shape=(out, out),
        in_specs=[smem_spec()] + [any_spec()] * 3,
        out_specs=(any_spec(), any_spec()),
        scratch_shapes=[
            pltpu.VMEM((days, width), BF16),
            pltpu.VMEM((2, rows, LANES), F32),
            pltpu.SemaphoreType.DMA((2,)),
            pltpu.SemaphoreType.DMA((2,)),
        ],
        compiler_params=params(),
        name="second_gram",
    )(place, ck, cr, after)


def bit_orders(bits):
    plain = list(range(bits))
    swapped = plain[:]
    if bits > 2:
        swapped[0], swapped[1] = 1, 0
    return plain, swapped


def cell_exchange(value, orders, stage, cells):
    pairs = []
    for c in range(cells):
        for d in range(2):
            pairs.append((2 * c + d, 2 * (c ^ (1 << orders[d][stage])) + d))
    return lax.ppermute(value, ("cell", "day"), pairs)


def other_core(value):
    return lax.ppermute(value, "day", [(0, 1), (1, 0)])


def sum_over_cells(keep, send):
    cells = lax.axis_size("cell")
    bits = cells.bit_length() - 1
    orders = bit_orders(bits)
    cell = lax.axis_index("cell")
    day = lax.axis_index("day")
    recv = other_core(send)
    mine = keep
    for stage in range(bits - 1):
        bit = jnp.where(day == 0, orders[0][stage], orders[1][stage])
        own = (cell >> bit) & 1
        half = mine.shape[0] // 2
        away = lax.dynamic_slice_in_dim(mine, (1 - own) * half, half, 0)
        away = away + lax.dynamic_slice_in_dim(recv, (1 - own) * half, half, 0)
        home = lax.dynamic_slice_in_dim(mine, own * half, half, 0)
        home = home + lax.dynamic_slice_in_dim(recv, own * half, half, 0)
        recv = cell_exchange(away, orders, stage, cells)
        mine = home
    part = mine + recv
    part = part + cell_exchange(part, orders, bits - 1, cells)
    for stage in reversed(range(bits - 1)):
        part = jnp.concatenate([part, cell_exchange(part, orders, stage, cells)], axis=0)
    return part


def placed_copies(source, target, half, bits, order, cell, sem):
    pieces = 1 << (bits - 1)
    rows = source.shape[0] // pieces
    copies = []
    for p in range(pieces):
        to = 0
        for stage in range(bits - 1):
            digit = (p >> (bits - 2 - stage)) & 1
            own = (cell >> order[stage]) & 1
            to = 2 * to + (own ^ digit)
        begin = pl.multiple_of(to * rows, 8)
        copies.append(
            pltpu.make_async_copy(
                source.at[pl.ds(p * rows, rows), :], target.at[half, pl.ds(begin, rows), :], sem.at[p]
            )
        )
    return copies


def load_block(packed, half, row, height, width):
    tiles = [packed[half, pl.ds(row + c * height, height), :] for c in range(width // LANES)]
    return jnp.concatenate(tiles, axis=1)


def split3(value):
    first = value.astype(BF16)
    rest = value - first.astype(F32)
    second = rest.astype(BF16)
    third = (rest - second.astype(F32)).astype(BF16)
    return first, second, third


def assemble(packed, half, row, i, j, gram):
    value = load_block(packed, half, row, BLOCK, BLOCK)
    rows, cols = pl.ds(i * BLOCK, BLOCK), pl.ds(j * BLOCK, BLOCK)
    for s, piece in enumerate(split3(value)):
        gram[s, rows, cols] = piece
    if i != j:
        for s, piece in enumerate(split3(value.T)):
            gram[s, cols, rows] = piece


def exact_dot(left, right):
    return jnp.dot(left, right, precision=lax.Precision.HIGHEST, preferred_element_type=F32)


def inverse_factor(moments):
    size = moments.shape[0]
    row_ids = lax.broadcasted_iota(jnp.int32, (size, size), 0)
    col_ids = lax.broadcasted_iota(jnp.int32, (size, size), 1)
    work = jnp.concatenate([(row_ids == col_ids).astype(F32), moments], axis=1)
    shape = (SUB, 2 * size)
    sub = lax.broadcasted_iota(jnp.int32, shape, 0)
    rows = [work[SUB * i : SUB * i + SUB, :] for i in range(size // SUB)]
    out = []
    for b in range(size // SUB):
        lane = size + SUB * b
        head = rows[b]
        cols = [jnp.broadcast_to(head[:, lane + c : lane + c + 1], shape) for c in range(SUB)]
        entry = [[jnp.broadcast_to(cols[c][r : r + 1, :], shape) for c in range(r + 1)] for r in range(SUB)]
        y = [jnp.broadcast_to(head[r : r + 1, :], shape) for r in range(SUB)]
        inverse = []
        factor = [[None] * SUB for _ in range(SUB)]
        for k in range(SUB):
            inverse.append(1.0 / entry[k][k])
            for i in range(k + 1, SUB):
                factor[i][k] = entry[i][k] * inverse[k]
                for j in range(k + 1, i + 1):
                    entry[i][j] = entry[i][j] - factor[i][k] * entry[j][k]
                y[i] = y[i] - factor[i][k] * y[k]
        p = [y[k] * inverse[k] for k in range(SUB)]
        for i in reversed(range(SUB)):
            for k in range(i):
                p[k] = p[k] - factor[i][k] * p[i]
        for i in range(b + 1, size // SUB):
            terms = [jnp.broadcast_to(rows[i][:, lane + k : lane + k + 1], shape) * p[k] for k in range(SUB)]
            while len(terms) > 1:
                terms = [terms[t] + terms[t + 1] for t in range(0, len(terms), 2)]
            rows[i] = rows[i] - terms[0]
        result, pivot = y[0], entry[0][0]
        for k in range(1, SUB):
            result = jnp.where(sub == k, y[k], result)
            pivot = jnp.where(sub == k, entry[k][k], pivot)
        out.append(result * (1.0 / jnp.sqrt(pivot)))
    return jnp.concatenate(out, axis=0)[:, :size]


def half_step(scores, gram, cells):
    value = jnp.dot(scores, gram[0], preferred_element_type=F32)
    for s in range(1, SPLITS):
        value = value + jnp.dot(scores, gram[s], preferred_element_type=F32)
    moments = sum(
        lax.dot_general(piece, scores, NT, preferred_element_type=F32) for piece in split3(value)
    )
    inverse = inverse_factor(moments / cells)
    return inverse, exact_dot(inverse, value).astype(BF16)


def chain_kernel(
    blocks, bits, orders, counts, place,
    a_own, a_twin, y_own, y_twin, b_own, b_twin, pk, pr, ck, cr,
    pred_out, cell_out,
    alpha, other, beta, pred, cell, pred_gram, cell_gram, sems, data_sems,
):
    day, group, index = place[0], place[1], place[2]
    data = load_days(pk, pr, pred, day, data_sems.at[0]) + load_days(ck, cr, cell, day, data_sems.at[1])
    for copy in data:
        copy.start()

    def gather(core):
        own, twin = orders[core], orders[1 - core]
        copies = []
        for n, (source, target, half, order) in enumerate(
            (
                (a_own, alpha, core, own),
                (a_twin, alpha, 1 - core, twin),
                (y_own, other, core, own),
                (y_twin, other, 1 - core, twin),
                (b_own, beta, core, own),
                (b_twin, beta, 1 - core, twin),
            )
        ):
            copies += placed_copies(source, target, half, bits, order, index, sems.at[n])
        for copy in copies:
            copy.start()
        for copy in copies:
            copy.wait()

    @pl.when(day == 0)
    def _():
        gather(0)

    @pl.when(day == 1)
    def _():
        gather(1)

    size = BLOCK * BLOCK // LANES
    share = len(blocks) // 2
    per_half = (share + 1) // 2

    def assemble_pred(mine, theirs):
        for g, packed in enumerate((mine, theirs)):
            for k in range(share):
                i, j = blocks[g * share + k]
                assemble(packed, k // per_half, (k % per_half) * size, i, j, pred_gram)

    @pl.when(group == 0)
    def _():
        assemble_pred(alpha, other)

    @pl.when(group == 1)
    def _():
        assemble_pred(other, alpha)

    for k, (i, j) in enumerate(blocks):
        assemble(beta, k // share, (k % share) * size, i, j, cell_gram)

    days = pred.shape[0]
    height = pred_out.shape[0]
    scores = load_block(alpha, 1, (share % per_half) * size, height, days).astype(BF16)
    pred_inverse = cell_inverse = pred_scores = loadings = None
    for _ in range(ITERS):
        pred_scores = scores
        pred_inverse, loadings = half_step(scores, pred_gram, counts[0])
        cell_inverse, scores = half_step(loadings, cell_gram, counts[1])
    for copy in data:
        copy.wait()
    raw = jnp.dot(pred_scores, pred[...], preferred_element_type=F32)
    pred_out[...] = exact_dot(pred_inverse, raw)
    raw = jnp.dot(loadings, cell[...], preferred_element_type=F32)
    cell_out[...] = exact_dot(cell_inverse, raw)


def local(predictors, predictand, pred_map, cell_map, start_panel):
    cells = lax.axis_size("cell")
    bits = cells.bit_length() - 1
    orders = bit_orders(bits)
    days = predictors.shape[0] * 2
    width = predictors.shape[1] // 2
    height = start_panel.shape[0]
    counts = (float(predictors.shape[1] * cells), float(predictand.shape[1] * cells))
    blocks = triangle(days)
    place = jnp.stack([lax.axis_index("day"), lax.axis_index("group"), lax.axis_index("cell")])
    place = place.astype(jnp.int32)

    pk, ps, ck, cs = place_tiles(place, pred_map, cell_map, predictors, predictand)
    pr = other_core(ps)
    cr = other_core(cs)
    a_keep, a_send = first_gram(place, pk, pr, ck, cr, start_panel)
    b_keep, b_send = second_gram(place, ck, cr, a_keep)
    a_own = sum_over_cells(a_keep, a_send)
    y_own = lax.ppermute(a_own, "group", [(0, 1), (1, 0)])
    b_own = sum_over_cells(b_keep, b_send)
    a_twin = other_core(a_own)
    y_twin = other_core(y_own)
    b_twin = other_core(b_own)

    out = jax.ShapeDtypeStruct((height, width), F32)
    pieces = 1 << (bits - 1)
    return pl.pallas_call(
        functools.partial(chain_kernel, blocks, bits, orders, counts),
        out_shape=(out, out),
        in_specs=[smem_spec()] + [any_spec()] * 10,
        scratch_shapes=[
            pltpu.VMEM((2,) + a_own.shape, F32),
            pltpu.VMEM((2,) + a_own.shape, F32),
            pltpu.VMEM((2,) + b_own.shape, F32),
            pltpu.VMEM((days, width), BF16),
            pltpu.VMEM((days, width), BF16),
            pltpu.VMEM((SPLITS, days, days), BF16),
            pltpu.VMEM((SPLITS, days, days), BF16),
            pltpu.SemaphoreType.DMA((6, pieces)),
            pltpu.SemaphoreType.DMA((2, 2)),
        ],
        compiler_params=params(),
        name="chain",
    )(place, a_own, a_twin, y_own, y_twin, b_own, b_twin, pk, pr, ck, cr)


def solution(mesh):
    in_specs = (
        P("day", "cell"),
        P("day", ("group", "cell")),
        P("cell"),
        P(("group", "cell")),
        P(None, ("group", "cell")),
    )
    out_specs = (P(None, ("group", "cell", "day")), P(None, ("group", "cell", "day")))
    return jax.shard_map(local, mesh=mesh, in_specs=in_specs, out_specs=out_specs, check_vma=False)
```

```python
import functools

import jax
import jax.numpy as jnp
from jax import lax
from jax.experimental import pallas as pl
from jax.experimental.pallas import tpu as pltpu
from jax.sharding import PartitionSpec as P

ITERS = 3
LANES = 128
UNIT = 128
SPLITS = 3
SUB = 8
F32 = jnp.float32
BF16 = jnp.bfloat16
NT = (((1,), (1,)), ((), ()))
VMEM_BYTES = 56 * 1024 * 1024


def own_blocks(count):
    return [(i, j) for i in range(count) for j in range(i, count)]


def shares(count):
    own = own_blocks(count)
    cross = [(i, j) for i in range(count) for j in range(count // 2)]
    return [
        (own[: len(own) // 2], cross[: len(cross) // 2]),
        (own[len(own) // 2 :], cross[len(cross) // 2 :]),
    ]


def padded(rows, bits):
    step = SUB << (bits - 1)
    return -(-rows // step) * step


def first_rows(count, height, bits):
    own, cross = shares(count)[0]
    return padded((len(own) + len(cross)) * UNIT + count * height, bits)


def second_rows(count, bits):
    return padded((len(own_blocks(count)) + count * (count // 2)) * UNIT, bits)


def any_spec():
    return pl.BlockSpec(memory_space=pl.ANY)


def smem_spec():
    return pl.BlockSpec(memory_space=pltpu.SMEM)


def params():
    return pltpu.CompilerParams(vmem_limit_bytes=VMEM_BYTES)


def start_all(copies):
    for copy in copies:
        copy.start()


def wait_all(copies):
    for copy in copies:
        copy.wait()


def load_days(keep, recv, whole, day, sems):
    rows = keep.shape[0]
    return [
        pltpu.make_async_copy(keep, whole.at[pl.ds(pl.multiple_of(day * rows, rows), rows), :], sems.at[0]),
        pltpu.make_async_copy(recv, whole.at[pl.ds(pl.multiple_of((1 - day) * rows, rows), rows), :], sems.at[1]),
    ]


def first_bit(orders, day, cell):
    return jnp.where(day == 0, (cell >> orders[0][0]) & 1, (cell >> orders[1][0]) & 1)


def flush(scr, home, away, bit, sems):
    rows = home.shape[0]
    copies = [
        pltpu.make_async_copy(scr.at[pl.ds(pl.multiple_of((1 - bit) * rows, SUB), rows), :], away, sems.at[0]),
        pltpu.make_async_copy(scr.at[pl.ds(pl.multiple_of(bit * rows, SUB), rows), :], home, sems.at[1]),
    ]
    start_all(copies)
    wait_all(copies)


def rows_at(whole, block):
    return whole[pl.ds(pl.multiple_of(block * UNIT, UNIT), UNIT), :]


def first_gram_kernel(orders, place, cell_map, pred_own, pred_recv, cell_own, start, home, away,
                      pred, cell, panel, scr, sems, tile_sems, outs):
    day, group, index = place[0], place[1], place[2]
    number = cell_map.shape[0]
    height = panel.shape[0]
    tiles = []
    for t in range(number):
        slot = pl.multiple_of(lax.rem(cell_map[t], number) * LANES, LANES)
        tiles.append(
            pltpu.make_async_copy(
                start.at[:, pl.ds(slot, LANES)], panel.at[:, pl.ds(t * LANES, LANES)], tile_sems.at[t]
            )
        )
    data = load_days(pred_own, pred_recv, pred, day, sems)
    field = pltpu.make_async_copy(cell_own, cell, sems.at[2])
    start_all(data)
    field.start()
    start_all(tiles)
    count = cell.shape[0] // UNIT
    (own0, cross0), (own1, cross1) = shares(count)
    row = 0
    wait_all(data)
    for (i0, j0), (i1, j1) in zip(own0, own1):
        left = rows_at(pred, day * count + i0 + group * (i1 - i0))
        right = rows_at(pred, day * count + j0 + group * (j1 - j0))
        scr[row : row + UNIT, :] = lax.dot_general(left, right, NT, preferred_element_type=F32)
        row += UNIT
    for (i0, j0), (i1, j1) in zip(cross0, cross1):
        left = rows_at(pred, i0 + group * (i1 - i0))
        right = rows_at(pred, count + day * (count // 2) + j0 + group * (j1 - j0))
        scr[row : row + UNIT, :] = lax.dot_general(left, right, NT, preferred_element_type=F32)
        row += UNIT
    field.wait()
    wait_all(tiles)
    scores = lax.dot_general(panel[...], cell[...], NT, preferred_element_type=F32)
    for c in range(count):
        scr[row : row + height, :] = scores[:, c * LANES : (c + 1) * LANES]
        row += height
    flush(scr, home, away, first_bit(orders, day, index), outs)


def second_gram_kernel(orders, place, cell_own, cell_recv, after, home, away, cell, scr, sems, outs):
    day, index = place[0], place[2]
    data = load_days(cell_own, cell_recv, cell, day, sems)
    start_all(data)
    wait_all(data)
    rows = cell_own.shape[0]
    count = rows // UNIT
    row = 0
    base = pl.multiple_of(day * rows, rows)
    for i in range(count):
        width = (count - i) * UNIT
        right = cell[pl.ds(base + i * UNIT, width), :]
        value = lax.dot_general(right[:UNIT, :], right, NT, preferred_element_type=F32)
        for c in range(count - i):
            scr[row : row + UNIT, :] = value[:, c * UNIT : (c + 1) * UNIT]
            row += UNIT
    side = rows // 2
    right = cell[pl.ds(rows + pl.multiple_of(day * side, side), side), :]
    value = lax.dot_general(cell[:rows, :], right, NT, preferred_element_type=F32)
    for i in range(count):
        for j in range(count // 2):
            scr[row : row + UNIT, :] = value[i * UNIT : (i + 1) * UNIT, j * UNIT : (j + 1) * UNIT]
            row += UNIT
    flush(scr, home, away, first_bit(orders, day, index), outs)


def first_gram(orders, bits, place, cell_map, pred_own, pred_recv, cell_own, start):
    rows, width = pred_own.shape
    height = start.shape[0]
    total = first_rows(rows // UNIT, height, bits)
    out = jax.ShapeDtypeStruct((total // 2, LANES), F32)
    return pl.pallas_call(
        functools.partial(first_gram_kernel, orders),
        out_shape=(out, out),
        in_specs=[smem_spec()] * 2 + [any_spec()] * 4,
        out_specs=(any_spec(), any_spec()),
        scratch_shapes=[
            pltpu.VMEM((2 * rows, width), BF16),
            pltpu.VMEM((rows, width), BF16),
            pltpu.VMEM((height, width), BF16),
            pltpu.VMEM((total, LANES), F32),
            pltpu.SemaphoreType.DMA((3,)),
            pltpu.SemaphoreType.DMA((cell_map.shape[0],)),
            pltpu.SemaphoreType.DMA((2,)),
        ],
        compiler_params=params(),
        name="first_gram",
    )(place, cell_map, pred_own, pred_recv, cell_own, start)


def second_gram(orders, bits, place, cell_own, cell_recv, after):
    rows, width = cell_own.shape
    total = second_rows(rows // UNIT, bits)
    out = jax.ShapeDtypeStruct((total // 2, LANES), F32)
    return pl.pallas_call(
        functools.partial(second_gram_kernel, orders),
        out_shape=(out, out),
        in_specs=[smem_spec()] + [any_spec()] * 3,
        out_specs=(any_spec(), any_spec()),
        scratch_shapes=[
            pltpu.VMEM((2 * rows, width), BF16),
            pltpu.VMEM((total, LANES), F32),
            pltpu.SemaphoreType.DMA((2,)),
            pltpu.SemaphoreType.DMA((2,)),
        ],
        compiler_params=params(),
        name="second_gram",
    )(place, cell_own, cell_recv, after)


def bit_orders(bits):
    plain = list(range(bits))
    swapped = plain[:]
    if bits > 2:
        swapped[0], swapped[1] = 1, 0
    return plain, swapped


def cell_exchange(value, orders, stage, cells):
    pairs = []
    for c in range(cells):
        for d in range(2):
            pairs.append((2 * c + d, 2 * (c ^ (1 << orders[d][stage])) + d))
    return lax.ppermute(value, ("cell", "day"), pairs)


def other_core(value):
    return lax.ppermute(value, "day", [(0, 1), (1, 0)])


def halve(orders, stage, mine, recv):
    bit = jnp.where(lax.axis_index("day") == 0, orders[0][stage], orders[1][stage])
    own = (lax.axis_index("cell") >> bit) & 1
    half = mine.shape[0] // 2
    away = lax.dynamic_slice_in_dim(mine, (1 - own) * half, half, 0)
    away = away + lax.dynamic_slice_in_dim(recv, (1 - own) * half, half, 0)
    home = lax.dynamic_slice_in_dim(mine, own * half, half, 0)
    home = home + lax.dynamic_slice_in_dim(recv, own * half, half, 0)
    return home, away


def finish_sum(orders, bits, cells, home, recv):
    for stage in range(1, bits - 1):
        home, away = halve(orders, stage, home, recv)
        recv = cell_exchange(away, orders, stage, cells)
    part = home + recv
    part = part + cell_exchange(part, orders, bits - 1, cells)
    for stage in reversed(range(bits - 1)):
        part = jnp.concatenate([part, cell_exchange(part, orders, stage, cells)], axis=0)
    return part


def placed_copies(source, target, half, bits, order, cell, sem):
    pieces = 1 << (bits - 1)
    rows = source.shape[0] // pieces
    copies = []
    for p in range(pieces):
        to = 0
        for stage in range(bits - 1):
            digit = (p >> (bits - 2 - stage)) & 1
            own = (cell >> order[stage]) & 1
            to = 2 * to + (own ^ digit)
        begin = pl.multiple_of(to * rows, SUB)
        copies.append(
            pltpu.make_async_copy(
                source.at[pl.ds(p * rows, rows), :], target.at[half, pl.ds(begin, rows), :], sem.at[p]
            )
        )
    return copies


def collect(day, cell, bits, orders, arrays, sems):
    def run(core):
        copies = []
        for n, (own, twin, target) in enumerate(arrays):
            copies += placed_copies(own, target, core, bits, orders[core], cell, sems.at[2 * n])
            copies += placed_copies(twin, target, 1 - core, bits, orders[1 - core], cell, sems.at[2 * n + 1])
        start_all(copies)
        wait_all(copies)

    @pl.when(day == 0)
    def _():
        run(0)

    @pl.when(day == 1)
    def _():
        run(1)


def split3(value):
    first = value.astype(BF16)
    rest = value - first.astype(F32)
    second = rest.astype(BF16)
    third = (rest - second.astype(F32)).astype(BF16)
    return first, second, third


def assemble(value, i, j, gram):
    rows, cols = pl.ds(i * UNIT, UNIT), pl.ds(j * UNIT, UNIT)
    for s, piece in enumerate(split3(value)):
        gram[s, rows, cols] = piece
    if i != j:
        for s, piece in enumerate(split3(value.T)):
            gram[s, cols, rows] = piece


def assemble_list(packed, core, count, own, cross, gram):
    row = 0
    for i, j in own:
        assemble(packed[core, row : row + UNIT, :], core * count + i, core * count + j, gram)
        row += UNIT
    for i, j in cross:
        assemble(packed[core, row : row + UNIT, :], i, count + core * (count // 2) + j, gram)
        row += UNIT
    return row


def exact_dot(left, right):
    return jnp.dot(left, right, precision=lax.Precision.HIGHEST, preferred_element_type=F32)


def inverse_factor(moments):
    size = moments.shape[0]
    row_ids = lax.broadcasted_iota(jnp.int32, (size, size), 0)
    col_ids = lax.broadcasted_iota(jnp.int32, (size, size), 1)
    work = jnp.concatenate([(row_ids == col_ids).astype(F32), moments], axis=1)
    shape = (SUB, 2 * size)
    sub = lax.broadcasted_iota(jnp.int32, shape, 0)
    rows = [work[SUB * i : SUB * i + SUB, :] for i in range(size // SUB)]
    out = []
    for b in range(size // SUB):
        lane = size + SUB * b
        head = rows[b]
        cols = [jnp.broadcast_to(head[:, lane + c : lane + c + 1], shape) for c in range(SUB)]
        entry = [[jnp.broadcast_to(cols[c][r : r + 1, :], shape) for c in range(r + 1)] for r in range(SUB)]
        y = [jnp.broadcast_to(head[r : r + 1, :], shape) for r in range(SUB)]
        inverse = []
        factor = [[None] * SUB for _ in range(SUB)]
        for k in range(SUB):
            inverse.append(1.0 / entry[k][k])
            for i in range(k + 1, SUB):
                factor[i][k] = entry[i][k] * inverse[k]
                for j in range(k + 1, i + 1):
                    entry[i][j] = entry[i][j] - factor[i][k] * entry[j][k]
                y[i] = y[i] - factor[i][k] * y[k]
        p = [y[k] * inverse[k] for k in range(SUB)]
        for i in reversed(range(SUB)):
            for k in range(i):
                p[k] = p[k] - factor[i][k] * p[i]
        for i in range(b + 1, size // SUB):
            terms = [jnp.broadcast_to(rows[i][:, lane + k : lane + k + 1], shape) * p[k] for k in range(SUB)]
            while len(terms) > 1:
                terms = [terms[t] + terms[t + 1] for t in range(0, len(terms), 2)]
            rows[i] = rows[i] - terms[0]
        result, pivot = y[0], entry[0][0]
        for k in range(1, SUB):
            result = jnp.where(sub == k, y[k], result)
            pivot = jnp.where(sub == k, entry[k][k], pivot)
        out.append(result * (1.0 / jnp.sqrt(pivot)))
    return jnp.concatenate(out, axis=0)[:, :size]


def half_step(scores, gram, cells):
    value = jnp.dot(scores, gram[0], preferred_element_type=F32)
    for s in range(1, SPLITS):
        value = value + jnp.dot(scores, gram[s], preferred_element_type=F32)
    moments = sum(
        lax.dot_general(piece, scores, NT, preferred_element_type=F32) for piece in split3(value)
    )
    return inverse_factor(moments / cells), value


def next_scores(inverse, value):
    return exact_dot(inverse, value).astype(BF16)


def first_chain_kernel(bits, orders, counts, place, a_own, a_twin, y_own, y_twin,
                       gram_out, scores_out, loadings_out, alpha, other, gram, sems, out_sem):
    day, group, index = place[0], place[1], place[2]
    collect(day, index, bits, orders, ((a_own, a_twin, alpha), (y_own, y_twin, other)), sems)
    days = gram.shape[1]
    count = days // UNIT // 2
    height = scores_out.shape[0]

    def assemble_all(packs):
        for packed, (own, cross) in zip(packs, shares(count)):
            for core in range(2):
                assemble_list(packed, core, count, own, cross, gram)

    @pl.when(group == 0)
    def _():
        assemble_all((alpha, other))

    @pl.when(group == 1)
    def _():
        assemble_all((other, alpha))

    save = pltpu.make_async_copy(gram, gram_out, out_sem)
    save.start()
    own, cross = shares(count)[0]
    begin = (len(own) + len(cross)) * UNIT
    tiles = [
        alpha[core, begin + c * height : begin + (c + 1) * height, :] for core in range(2) for c in range(count)
    ]
    scores = jnp.concatenate(tiles, axis=1).astype(BF16)
    scores_out[...] = scores
    inverse, value = half_step(scores, gram, counts[0])
    loadings_out[...] = next_scores(inverse, value)
    save.wait()


def first_chain(bits, orders, counts, days, height, place, a_own, a_twin, y_own, y_twin):
    pieces = 1 << (bits - 1)
    vmem = pl.BlockSpec(memory_space=pltpu.VMEM)
    panel = jax.ShapeDtypeStruct((height, days), BF16)
    return pl.pallas_call(
        functools.partial(first_chain_kernel, bits, orders, counts),
        out_shape=(jax.ShapeDtypeStruct((SPLITS, days, days), BF16), panel, panel),
        in_specs=[smem_spec()] + [any_spec()] * 4,
        out_specs=(any_spec(), vmem, vmem),
        scratch_shapes=[
            pltpu.VMEM((2,) + a_own.shape, F32),
            pltpu.VMEM((2,) + a_own.shape, F32),
            pltpu.VMEM((SPLITS, days, days), BF16),
            pltpu.SemaphoreType.DMA((4, pieces)),
            pltpu.SemaphoreType.DMA,
        ],
        compiler_params=params(),
        name="first_chain",
    )(place, a_own, a_twin, y_own, y_twin)


def load_tiles(tile_map, own, recv, whole, day, sems):
    number = tile_map.shape[0]
    half = number // 2
    rows = own.shape[0]
    mine = pl.ds(pl.multiple_of(day * rows, rows), rows)
    theirs = pl.ds(pl.multiple_of((1 - day) * rows, rows), rows)
    for t in range(number):
        slot = lax.rem(tile_map[t], number)
        place = lax.rem(slot, half)
        to = pl.ds(pl.multiple_of(place * LANES, LANES), LANES)
        source = pl.ds(t * LANES, LANES)

        @pl.when(lax.div(slot, half) == day)
        def _():
            pltpu.make_async_copy(own.at[:, source], whole.at[mine, to], sems.at[0, place]).start()
            pltpu.make_async_copy(recv.at[:, source], whole.at[theirs, to], sems.at[1, place]).start()


def wait_tiles(tile_map, own, whole, sems):
    rows = own.shape[0]
    part = pl.ds(0, LANES)
    for place in range(tile_map.shape[0] // 2):
        for n in range(2):
            pltpu.make_async_copy(own.at[:, part], whole.at[pl.ds(0, rows), part], sems.at[n, place]).wait()


def second_chain_kernel(bits, orders, counts, place, pred_map, cell_map, b_own, b_twin, gram_in, scores_in,
                        loadings_in, pred_own, pred_recv, cell_own, cell_recv, pred_out, cell_out,
                        beta, pred, cell, pred_gram, cell_gram, sems, gram_sem, pred_sems, cell_sems):
    day, index = place[0], place[2]
    restore = pltpu.make_async_copy(gram_in, pred_gram, gram_sem)
    collect(day, index, bits, orders, ((b_own, b_twin, beta),), sems)
    restore.start()
    load_tiles(pred_map, pred_own, pred_recv, pred, day, pred_sems)
    load_tiles(cell_map, cell_own, cell_recv, cell, day, cell_sems)
    days = pred.shape[0]
    count = days // UNIT // 2
    own = own_blocks(count)
    cross = [(i, j) for i in range(count) for j in range(count // 2)]
    for core in range(2):
        assemble_list(beta, core, count, own, cross, cell_gram)
    pred_scores, loadings = scores_in[...], loadings_in[...]
    pred_inverse = pred_value = None
    for iteration in range(ITERS):
        if iteration > 0 or ITERS == 1:
            pred_inverse, pred_value = half_step(pred_scores, pred_gram, counts[0])
            loadings = next_scores(pred_inverse, pred_value)
        cell_inverse, cell_value = half_step(loadings, cell_gram, counts[1])
        if iteration == 0:
            restore.wait()
            wait_tiles(pred_map, pred_own, pred, pred_sems)
            wait_tiles(cell_map, cell_own, cell, cell_sems)
        if iteration < ITERS - 1:
            pred_scores = next_scores(cell_inverse, cell_value)
    raw = jnp.dot(pred_scores, pred[...], preferred_element_type=F32)
    pred_out[...] = exact_dot(pred_inverse, raw)
    raw = jnp.dot(loadings, cell[...], preferred_element_type=F32)
    cell_out[...] = exact_dot(cell_inverse, raw)


def second_chain(bits, orders, counts, place, pred_map, cell_map, b_own, b_twin, gram, scores, loadings, fields):
    pieces = 1 << (bits - 1)
    height, days = scores.shape
    width = fields[0].shape[1] // 2
    tiles = pred_map.shape[0] // 2
    vmem = pl.BlockSpec(memory_space=pltpu.VMEM)
    out = jax.ShapeDtypeStruct((height, width), F32)
    return pl.pallas_call(
        functools.partial(second_chain_kernel, bits, orders, counts),
        out_shape=(out, out),
        in_specs=[smem_spec()] * 3 + [any_spec()] * 3 + [vmem] * 2 + [any_spec()] * 4,
        out_specs=(vmem, vmem),
        scratch_shapes=[
            pltpu.VMEM((2,) + b_own.shape, F32),
            pltpu.VMEM((days, width), BF16),
            pltpu.VMEM((days, width), BF16),
            pltpu.VMEM((SPLITS, days, days), BF16),
            pltpu.VMEM((SPLITS, days, days), BF16),
            pltpu.SemaphoreType.DMA((2, pieces)),
            pltpu.SemaphoreType.DMA,
            pltpu.SemaphoreType.DMA((2, tiles)),
            pltpu.SemaphoreType.DMA((2, tiles)),
        ],
        compiler_params=params(),
        name="second_chain",
    )(place, pred_map, cell_map, b_own, b_twin, gram, scores, loadings, *fields)


def local(predictors, predictand, pred_map, cell_map, start_panel):
    cells = lax.axis_size("cell")
    bits = cells.bit_length() - 1
    orders = bit_orders(bits)
    days = predictors.shape[0] * 2
    height = start_panel.shape[0]
    counts = (float(predictors.shape[1] * cells), float(predictand.shape[1] * cells))
    place = jnp.stack([lax.axis_index("day"), lax.axis_index("group"), lax.axis_index("cell")])
    place = place.astype(jnp.int32)

    pred_recv = other_core(predictors)
    cell_recv = other_core(predictand)
    a_home, a_away = first_gram(orders, bits, place, cell_map, predictors, pred_recv, predictand, start_panel)
    b_home, b_away = second_gram(orders, bits, place, predictand, cell_recv, a_away)
    a_recv = cell_exchange(a_away, orders, 0, cells)
    b_away, a_recv = lax.optimization_barrier((b_away, a_recv))
    a_own = finish_sum(orders, bits, cells, a_home, a_recv)
    b_recv = cell_exchange(b_away, orders, 0, cells)
    b_own = finish_sum(orders, bits, cells, b_home, b_recv)
    y_own = lax.ppermute(a_own, "group", [(0, 1), (1, 0)])
    a_twin = other_core(a_own)
    y_twin = other_core(y_own)
    b_twin = other_core(b_own)
    gram, scores, loadings = first_chain(
        bits, orders, counts, days, height, place, a_own, a_twin, y_own, y_twin
    )
    return second_chain(
        bits, orders, counts, place, pred_map, cell_map, b_own, b_twin, gram, scores, loadings,
        (predictors, pred_recv, predictand, cell_recv),
    )


def solution(mesh):
    in_specs = (
        P("day", "cell"),
        P("day", ("group", "cell")),
        P("cell"),
        P(("group", "cell")),
        P(None, ("group", "cell")),
    )
    out_specs = (P(None, ("group", "cell", "day")), P(None, ("group", "cell", "day")))
    return jax.shard_map(local, mesh=mesh, in_specs=in_specs, out_specs=out_specs, check_vma=False)
```

```python
import functools

import jax
import jax.numpy as jnp
from jax import lax
from jax.experimental import pallas as pl
from jax.experimental.pallas import tpu as pltpu
from jax.sharding import PartitionSpec as P

ITERS = 3
LANES = 128
UNIT = 128
SPLITS = 3
SUB = 8
F32 = jnp.float32
BF16 = jnp.bfloat16
NT = (((1,), (1,)), ((), ()))
VMEM_BYTES = 56 * 1024 * 1024


def own_blocks(count):
    return [(i, j) for i in range(count) for j in range(i, count)]


def shares(count):
    own = own_blocks(count)
    cross = [(i, j) for i in range(count) for j in range(count // 2)]
    return [
        (own[: len(own) // 2], cross[: len(cross) // 2]),
        (own[len(own) // 2 :], cross[len(cross) // 2 :]),
    ]


def padded(rows, bits):
    step = SUB << (bits - 1)
    return -(-rows // step) * step


def first_rows(count, height, bits):
    own, cross = shares(count)[0]
    return padded((len(own) + len(cross)) * UNIT + count * height, bits)


def second_rows(count, bits):
    return padded((len(own_blocks(count)) + count * (count // 2)) * UNIT, bits)


def any_spec():
    return pl.BlockSpec(memory_space=pl.ANY)


def smem_spec():
    return pl.BlockSpec(memory_space=pltpu.SMEM)


def params():
    return pltpu.CompilerParams(vmem_limit_bytes=VMEM_BYTES)


def start_all(copies):
    for copy in copies:
        copy.start()


def wait_all(copies):
    for copy in copies:
        copy.wait()


def first_bit(orders, day, cell):
    return jnp.where(day == 0, (cell >> orders[0][0]) & 1, (cell >> orders[1][0]) & 1)


def flush(scr, home, away, bit, sems):
    rows = home.shape[0]
    copies = [
        pltpu.make_async_copy(scr.at[pl.ds(pl.multiple_of((1 - bit) * rows, SUB), rows), :], away, sems.at[0]),
        pltpu.make_async_copy(scr.at[pl.ds(pl.multiple_of(bit * rows, SUB), rows), :], home, sems.at[1]),
    ]
    start_all(copies)
    wait_all(copies)


def own_gram_kernel(place, cell_map, pred_own, cell_own, start, first_out, second_out,
                    pred, cell, panel, first, second, sems, tile_sems, outs):
    group = place[1]
    number = cell_map.shape[0]
    height = panel.shape[0]
    loads = [pltpu.make_async_copy(cell_own, cell, sems.at[0]), pltpu.make_async_copy(pred_own, pred, sems.at[1])]
    tiles = []
    for t in range(number):
        slot = pl.multiple_of(lax.rem(cell_map[t], number) * LANES, LANES)
        tiles.append(
            pltpu.make_async_copy(
                start.at[:, pl.ds(slot, LANES)], panel.at[:, pl.ds(t * LANES, LANES)], tile_sems.at[t]
            )
        )
    start_all(tiles)
    start_all(loads)
    count = cell.shape[0] // UNIT
    loads[0].wait()
    row = 0
    for i in range(count):
        right = cell[i * UNIT :, :]
        value = lax.dot_general(right[:UNIT, :], right, NT, preferred_element_type=F32)
        for c in range(count - i):
            second[row : row + UNIT, :] = value[:, c * UNIT : (c + 1) * UNIT]
            row += UNIT
    save = pltpu.make_async_copy(second, second_out, outs.at[1])
    save.start()
    wait_all(tiles)
    row = 0
    scores = lax.dot_general(panel[...], cell[...], NT, preferred_element_type=F32)
    for c in range(count):
        first[row : row + height, :] = scores[:, c * LANES : (c + 1) * LANES]
        row += height
    loads[1].wait()
    for (i0, j0), (i1, j1) in zip(shares(count)[0][0], shares(count)[1][0]):
        left = rows_at(pred, i0 + group * (i1 - i0))
        right = rows_at(pred, j0 + group * (j1 - j0))
        first[row : row + UNIT, :] = lax.dot_general(left, right, NT, preferred_element_type=F32)
        row += UNIT
    last = pltpu.make_async_copy(first, first_out, outs.at[0])
    last.start()
    last.wait()
    save.wait()


def rows_at(whole, block):
    return whole[pl.ds(pl.multiple_of(block * UNIT, UNIT), UNIT), :]


def own_gram(place, cell_map, pred_own, cell_own, start):
    rows, width = pred_own.shape
    height = start.shape[0]
    count = rows // UNIT
    number = len(own_blocks(count))
    first = number // 2 * UNIT + count * height
    second = number * UNIT
    return pl.pallas_call(
        own_gram_kernel,
        out_shape=(jax.ShapeDtypeStruct((first, LANES), F32), jax.ShapeDtypeStruct((second, LANES), F32)),
        in_specs=[smem_spec()] * 2 + [any_spec()] * 3,
        out_specs=(any_spec(), any_spec()),
        scratch_shapes=[
            pltpu.VMEM((rows, width), BF16),
            pltpu.VMEM((rows, width), BF16),
            pltpu.VMEM((height, width), BF16),
            pltpu.VMEM((first, LANES), F32),
            pltpu.VMEM((second, LANES), F32),
            pltpu.SemaphoreType.DMA((2,)),
            pltpu.SemaphoreType.DMA((cell_map.shape[0],)),
            pltpu.SemaphoreType.DMA((2,)),
        ],
        compiler_params=params(),
        name="own_gram",
    )(place, cell_map, pred_own, cell_own, start)


def cross_gram_kernel(orders, shared, place, own, recv, part, home, away, left, right, scr, sems, outs):
    day, group, index = place[0], place[1], place[2]
    height, side = left.shape[0], right.shape[0]
    at_left = pl.ds(pl.multiple_of(group * height, height), height) if shared else pl.ds(0, height)
    at_right = pl.ds(pl.multiple_of(day * side, side), side)
    keep = pltpu.make_async_copy(part, scr.at[pl.ds(0, part.shape[0]), :], sems.at[2])
    keep.start()

    @pl.when(day == 0)
    def _():
        pltpu.make_async_copy(own.at[at_left, :], left, sems.at[0]).start()
        pltpu.make_async_copy(recv.at[at_right, :], right, sems.at[1]).start()

    @pl.when(day == 1)
    def _():
        pltpu.make_async_copy(recv.at[at_left, :], left, sems.at[0]).start()
        pltpu.make_async_copy(own.at[at_right, :], right, sems.at[1]).start()

    pltpu.make_async_copy(own.at[at_left, :], left, sems.at[0]).wait()
    pltpu.make_async_copy(own.at[at_right, :], right, sems.at[1]).wait()
    row = part.shape[0]
    for i in range(height // UNIT):
        value = lax.dot_general(
            left[i * UNIT : (i + 1) * UNIT, :], right[...], NT, preferred_element_type=F32
        )
        for j in range(side // UNIT):
            scr[row : row + UNIT, :] = value[:, j * UNIT : (j + 1) * UNIT]
            row += UNIT
    keep.wait()
    flush(scr, home, away, first_bit(orders, day, index), outs)


def cross_gram(orders, shared, total, name, place, own, recv, part):
    rows, width = own.shape
    out = jax.ShapeDtypeStruct((total // 2, LANES), F32)
    return pl.pallas_call(
        functools.partial(cross_gram_kernel, orders, shared),
        out_shape=(out, out),
        in_specs=[smem_spec()] + [any_spec()] * 3,
        out_specs=(any_spec(), any_spec()),
        scratch_shapes=[
            pltpu.VMEM((rows // 2 if shared else rows, width), BF16),
            pltpu.VMEM((rows // 2, width), BF16),
            pltpu.VMEM((total, LANES), F32),
            pltpu.SemaphoreType.DMA((3,)),
            pltpu.SemaphoreType.DMA((2,)),
        ],
        compiler_params=params(),
        name=name,
    )(place, own, recv, part)


def after(value, gate):
    return lax.optimization_barrier((value, gate))[0]


def bit_orders(bits):
    plain = list(range(bits))
    swapped = plain[:]
    if bits > 2:
        swapped[0], swapped[1] = 1, 0
    return plain, swapped


def cell_exchange(value, orders, stage, cells):
    pairs = []
    for c in range(cells):
        for d in range(2):
            pairs.append((2 * c + d, 2 * (c ^ (1 << orders[d][stage])) + d))
    return lax.ppermute(value, ("cell", "day"), pairs)


def other_core(value):
    return lax.ppermute(value, "day", [(0, 1), (1, 0)])


def other_group(value):
    return lax.ppermute(value, "group", [(0, 1), (1, 0)])


def halve(orders, stage, mine, recv):
    bit = jnp.where(lax.axis_index("day") == 0, orders[0][stage], orders[1][stage])
    own = (lax.axis_index("cell") >> bit) & 1
    half = mine.shape[0] // 2
    away = lax.dynamic_slice_in_dim(mine, (1 - own) * half, half, 0)
    away = away + lax.dynamic_slice_in_dim(recv, (1 - own) * half, half, 0)
    home = lax.dynamic_slice_in_dim(mine, own * half, half, 0)
    home = home + lax.dynamic_slice_in_dim(recv, own * half, half, 0)
    return home, away


def sum_chunks(orders, bits, cells, first, second):
    home, away = first
    late_home, late_away = second
    last = bits - 1
    recv = cell_exchange(away, orders, 0, cells)
    home, away = halve(orders, 1, home, recv)
    late_away = after(late_away, away)
    recv = cell_exchange(away, orders, 1, cells)
    late = cell_exchange(late_away, orders, 0, cells)
    for stage in range(2, last):
        home, away = halve(orders, stage, home, recv)
        recv = cell_exchange(away, orders, stage, cells)
    part = home + recv
    middle = cell_exchange(part, orders, last, cells)
    late_home, late_away = halve(orders, 1, late_home, after(late, part))
    late = cell_exchange(late_away, orders, 1, cells)
    for stage in range(2, last):
        late_home, late_away = halve(orders, stage, late_home, late)
        late = cell_exchange(late_away, orders, stage, cells)
    part = part + after(middle, late_away)
    late_part = after(late_home + late, part)
    for stage in reversed(range(1, last)):
        part = jnp.concatenate([part, cell_exchange(part, orders, stage, cells)], axis=0)
    late_middle = cell_exchange(late_part, orders, last, cells)
    other = other_group(part)
    rest = after(cell_exchange(part, orders, 0, cells), late_part)
    other_rest = other_group(rest)
    late_part = late_part + after(after(late_middle, rest), other)
    for stage in reversed(range(1, last)):
        recv = cell_exchange(late_part, orders, stage, cells)
        late_part = jnp.concatenate([late_part, recv if stage > 1 else after(recv, other_rest)], axis=0)
    late_rest = cell_exchange(late_part, orders, 0, cells)
    return (part, rest), (other, other_rest), (late_part, late_rest)


def placed_copies(sources, target, half, bits, order, cell, sem):
    pieces = 1 << (bits - 1)
    rows = target.shape[1] // pieces
    copies = []
    for p in range(pieces):
        to = 0
        for stage in range(bits - 1):
            digit = (p >> (bits - 2 - stage)) & 1
            own = (cell >> order[stage]) & 1
            to = 2 * to + (own ^ digit)
        begin = pl.multiple_of(to * rows, SUB)
        source = sources[p // (pieces // 2)]
        at = p % (pieces // 2) * rows
        copies.append(
            pltpu.make_async_copy(
                source.at[pl.ds(at, rows), :], target.at[half, pl.ds(begin, rows), :], sem.at[p]
            )
        )
    return copies


def collect(day, cell, bits, orders, arrays, sems):
    def run(core):
        copies = []
        for n, (own, twin, target) in enumerate(arrays):
            copies += placed_copies(own, target, core, bits, orders[core], cell, sems.at[2 * n])
            copies += placed_copies(twin, target, 1 - core, bits, orders[1 - core], cell, sems.at[2 * n + 1])
        start_all(copies)
        wait_all(copies)

    @pl.when(day == 0)
    def _():
        run(0)

    @pl.when(day == 1)
    def _():
        run(1)


def split3(value):
    first = value.astype(BF16)
    rest = value - first.astype(F32)
    second = rest.astype(BF16)
    third = (rest - second.astype(F32)).astype(BF16)
    return first, second, third


def assemble(value, i, j, gram):
    rows, cols = pl.ds(i * UNIT, UNIT), pl.ds(j * UNIT, UNIT)
    for s, piece in enumerate(split3(value)):
        gram[s, rows, cols] = piece
    if i != j:
        for s, piece in enumerate(split3(value.T)):
            gram[s, cols, rows] = piece


def assemble_list(packed, core, row, count, own, cross, gram):
    for i, j in own:
        assemble(packed[core, row : row + UNIT, :], core * count + i, core * count + j, gram)
        row += UNIT
    for i, j in cross:
        assemble(packed[core, row : row + UNIT, :], i, count + core * (count // 2) + j, gram)
        row += UNIT


def exact_dot(left, right):
    return jnp.dot(left, right, precision=lax.Precision.HIGHEST, preferred_element_type=F32)


def inverse_factor(moments):
    size = moments.shape[0]
    row_ids = lax.broadcasted_iota(jnp.int32, (size, size), 0)
    col_ids = lax.broadcasted_iota(jnp.int32, (size, size), 1)
    work = jnp.concatenate([(row_ids == col_ids).astype(F32), moments], axis=1)
    shape = (SUB, 2 * size)
    sub = lax.broadcasted_iota(jnp.int32, shape, 0)
    rows = [work[SUB * i : SUB * i + SUB, :] for i in range(size // SUB)]
    out = []
    for b in range(size // SUB):
        lane = size + SUB * b
        head = rows[b]
        cols = [jnp.broadcast_to(head[:, lane + c : lane + c + 1], shape) for c in range(SUB)]
        entry = [[jnp.broadcast_to(cols[c][r : r + 1, :], shape) for c in range(r + 1)] for r in range(SUB)]
        y = [jnp.broadcast_to(head[r : r + 1, :], shape) for r in range(SUB)]
        inverse = []
        factor = [[None] * SUB for _ in range(SUB)]
        for k in range(SUB):
            inverse.append(1.0 / entry[k][k])
            for i in range(k + 1, SUB):
                factor[i][k] = entry[i][k] * inverse[k]
                for j in range(k + 1, i + 1):
                    entry[i][j] = entry[i][j] - factor[i][k] * entry[j][k]
                y[i] = y[i] - factor[i][k] * y[k]
        p = [y[k] * inverse[k] for k in range(SUB)]
        for i in reversed(range(SUB)):
            for k in range(i):
                p[k] = p[k] - factor[i][k] * p[i]
        for i in range(b + 1, size // SUB):
            terms = [jnp.broadcast_to(rows[i][:, lane + k : lane + k + 1], shape) * p[k] for k in range(SUB)]
            while len(terms) > 1:
                terms = [terms[t] + terms[t + 1] for t in range(0, len(terms), 2)]
            rows[i] = rows[i] - terms[0]
        result, pivot = y[0], entry[0][0]
        for k in range(1, SUB):
            result = jnp.where(sub == k, y[k], result)
            pivot = jnp.where(sub == k, entry[k][k], pivot)
        out.append(result * (1.0 / jnp.sqrt(pivot)))
    return jnp.concatenate(out, axis=0)[:, :size]


def half_step(scores, gram, cells):
    value = jnp.dot(scores, gram[0], preferred_element_type=F32)
    for s in range(1, SPLITS):
        value = value + jnp.dot(scores, gram[s], preferred_element_type=F32)
    moments = sum(
        lax.dot_general(piece, scores, NT, preferred_element_type=F32) for piece in split3(value)
    )
    return inverse_factor(moments / cells), value


def next_scores(inverse, value):
    return exact_dot(inverse, value).astype(BF16)


def first_chain_kernel(bits, orders, counts, place, a0, a1, y0, y1, a0_twin, a1_twin, y0_twin, y1_twin,
                       gram_out, scores_out, loadings_out, alpha, other, gram, sems, out_sem):
    day, group, index = place[0], place[1], place[2]
    arrays = (((a0, a1), (a0_twin, a1_twin), alpha), ((y0, y1), (y0_twin, y1_twin), other))
    collect(day, index, bits, orders, arrays, sems)
    days = gram.shape[1]
    count = days // UNIT // 2
    height = scores_out.shape[0]

    def assemble_all(packs):
        for packed, (own, cross) in zip(packs, shares(count)):
            for core in range(2):
                assemble_list(packed, core, count * height, count, own, cross, gram)

    @pl.when(group == 0)
    def _():
        assemble_all((alpha, other))

    @pl.when(group == 1)
    def _():
        assemble_all((other, alpha))

    save = pltpu.make_async_copy(gram, gram_out, out_sem)
    save.start()
    tiles = [alpha[core, c * height : (c + 1) * height, :] for core in range(2) for c in range(count)]
    scores = jnp.concatenate(tiles, axis=1).astype(BF16)
    scores_out[...] = scores
    inverse, value = half_step(scores, gram, counts[0])
    loadings_out[...] = next_scores(inverse, value)
    save.wait()


def first_chain(bits, orders, counts, days, height, place, sums):
    pieces = 1 << (bits - 1)
    vmem = pl.BlockSpec(memory_space=pltpu.VMEM)
    panel = jax.ShapeDtypeStruct((height, days), BF16)
    return pl.pallas_call(
        functools.partial(first_chain_kernel, bits, orders, counts),
        out_shape=(jax.ShapeDtypeStruct((SPLITS, days, days), BF16), panel, panel),
        in_specs=[smem_spec()] + [any_spec()] * 8,
        out_specs=(any_spec(), vmem, vmem),
        scratch_shapes=[
            pltpu.VMEM((2, 2 * sums[0].shape[0], LANES), F32),
            pltpu.VMEM((2, 2 * sums[0].shape[0], LANES), F32),
            pltpu.VMEM((SPLITS, days, days), BF16),
            pltpu.SemaphoreType.DMA((4, pieces)),
            pltpu.SemaphoreType.DMA,
        ],
        compiler_params=params(),
        name="first_chain",
    )(place, *sums)


def load_tiles(tile_map, own, recv, whole, day, sems):
    number = tile_map.shape[0]
    half = number // 2
    rows = own.shape[0]
    mine = pl.ds(pl.multiple_of(day * rows, rows), rows)
    theirs = pl.ds(pl.multiple_of((1 - day) * rows, rows), rows)
    for t in range(number):
        slot = lax.rem(tile_map[t], number)
        place = lax.rem(slot, half)
        to = pl.ds(pl.multiple_of(place * LANES, LANES), LANES)
        source = pl.ds(t * LANES, LANES)

        @pl.when(lax.div(slot, half) == day)
        def _():
            pltpu.make_async_copy(own.at[:, source], whole.at[mine, to], sems.at[0, place]).start()
            pltpu.make_async_copy(recv.at[:, source], whole.at[theirs, to], sems.at[1, place]).start()


def wait_tiles(tile_map, own, whole, sems):
    rows = own.shape[0]
    part = pl.ds(0, LANES)
    for place in range(tile_map.shape[0] // 2):
        for n in range(2):
            pltpu.make_async_copy(own.at[:, part], whole.at[pl.ds(0, rows), part], sems.at[n, place]).wait()


def second_chain_kernel(bits, orders, counts, place, pred_map, cell_map, b0, b1, b0_twin, b1_twin, gram_in, scores_in,
                        loadings_in, pred_own, pred_recv, cell_own, cell_recv, pred_out, cell_out,
                        beta, pred, cell, pred_gram, cell_gram, sems, gram_sem, pred_sems, cell_sems):
    day, index = place[0], place[2]
    restore = pltpu.make_async_copy(gram_in, pred_gram, gram_sem)
    collect(day, index, bits, orders, (((b0, b1), (b0_twin, b1_twin), beta),), sems)
    restore.start()
    load_tiles(pred_map, pred_own, pred_recv, pred, day, pred_sems)
    load_tiles(cell_map, cell_own, cell_recv, cell, day, cell_sems)
    days = pred.shape[0]
    count = days // UNIT // 2
    own = own_blocks(count)
    cross = [(i, j) for i in range(count) for j in range(count // 2)]
    for core in range(2):
        assemble_list(beta, core, 0, count, own, cross, cell_gram)
    pred_scores, loadings = scores_in[...], loadings_in[...]
    pred_inverse = pred_value = None
    for iteration in range(ITERS):
        if iteration > 0 or ITERS == 1:
            pred_inverse, pred_value = half_step(pred_scores, pred_gram, counts[0])
            loadings = next_scores(pred_inverse, pred_value)
        cell_inverse, cell_value = half_step(loadings, cell_gram, counts[1])
        if iteration == 0:
            restore.wait()
            wait_tiles(pred_map, pred_own, pred, pred_sems)
            wait_tiles(cell_map, cell_own, cell, cell_sems)
        if iteration < ITERS - 1:
            pred_scores = next_scores(cell_inverse, cell_value)
    raw = jnp.dot(pred_scores, pred[...], preferred_element_type=F32)
    pred_out[...] = exact_dot(pred_inverse, raw)
    raw = jnp.dot(loadings, cell[...], preferred_element_type=F32)
    cell_out[...] = exact_dot(cell_inverse, raw)


def second_chain(bits, orders, counts, place, pred_map, cell_map, sums, gram, scores, loadings, fields):
    pieces = 1 << (bits - 1)
    height, days = scores.shape
    width = fields[0].shape[1] // 2
    tiles = pred_map.shape[0] // 2
    vmem = pl.BlockSpec(memory_space=pltpu.VMEM)
    out = jax.ShapeDtypeStruct((height, width), F32)
    return pl.pallas_call(
        functools.partial(second_chain_kernel, bits, orders, counts),
        out_shape=(out, out),
        in_specs=[smem_spec()] * 3 + [any_spec()] * 5 + [vmem] * 2 + [any_spec()] * 4,
        out_specs=(vmem, vmem),
        scratch_shapes=[
            pltpu.VMEM((2, 2 * sums[0].shape[0], LANES), F32),
            pltpu.VMEM((days, width), BF16),
            pltpu.VMEM((days, width), BF16),
            pltpu.VMEM((SPLITS, days, days), BF16),
            pltpu.VMEM((SPLITS, days, days), BF16),
            pltpu.SemaphoreType.DMA((2, pieces)),
            pltpu.SemaphoreType.DMA,
            pltpu.SemaphoreType.DMA((2, tiles)),
            pltpu.SemaphoreType.DMA((2, tiles)),
        ],
        compiler_params=params(),
        name="second_chain",
    )(place, pred_map, cell_map, *sums, gram, scores, loadings, *fields)


def local(predictors, predictand, pred_map, cell_map, start_panel):
    cells = lax.axis_size("cell")
    bits = cells.bit_length() - 1
    orders = bit_orders(bits)
    days = predictors.shape[0] * 2
    height = start_panel.shape[0]
    counts = (float(predictors.shape[1] * cells), float(predictand.shape[1] * cells))
    place = jnp.stack([lax.axis_index("day"), lax.axis_index("group"), lax.axis_index("cell")])
    place = place.astype(jnp.int32)

    pred_recv = other_core(predictors)
    cell_recv = other_core(predictand)
    count = predictors.shape[0] // UNIT
    first_part, second_part = own_gram(place, cell_map, predictors, predictand, start_panel)
    first = cross_gram(
        orders, True, first_rows(count, height, bits), "first_cross", place, predictors, pred_recv, first_part
    )
    second = cross_gram(
        orders, False, second_rows(count, bits), "second_cross", place, predictand, after(cell_recv, first[1]), second_part
    )
    mine, other, late = sum_chunks(orders, bits, cells, first, second)
    sums = mine + other
    gram, scores, loadings = first_chain(
        bits, orders, counts, days, height, place, sums + tuple(other_core(part) for part in sums)
    )
    late = (late[0], after(late[1], loadings))
    late = late + tuple(other_core(part) for part in late)
    return second_chain(
        bits, orders, counts, place, pred_map, cell_map, late, gram, scores, loadings,
        (predictors, pred_recv, predictand, cell_recv),
    )


def solution(mesh):
    in_specs = (
        P("day", "cell"),
        P("day", ("group", "cell")),
        P("cell"),
        P(("group", "cell")),
        P(None, ("group", "cell")),
    )
    out_specs = (P(None, ("group", "cell", "day")), P(None, ("group", "cell", "day")))
    return jax.shard_map(local, mesh=mesh, in_specs=in_specs, out_specs=out_specs, check_vma=False)
```

```python
import functools

import jax
import jax.numpy as jnp
from jax import lax
from jax.experimental import pallas as pl
from jax.experimental.pallas import tpu as pltpu
from jax.sharding import PartitionSpec as P

ITERS = 3
LANES = 128
UNIT = 128
SPLITS = 3
SUB = 8
F32 = jnp.float32
BF16 = jnp.bfloat16
NT = (((1,), (1,)), ((), ()))
MIB = 1024 * 1024


def own_blocks(count):
    return [(i, j) for i in range(count) for j in range(i, count)]


def shares(count):
    own = own_blocks(count)
    cross = [(i, j) for i in range(count) for j in range(count // 2)]
    return [
        (own[: len(own) // 2], cross[: len(cross) // 2]),
        (own[len(own) // 2 :], cross[len(cross) // 2 :]),
    ]


def padded(rows, bits):
    step = SUB << (bits - 1)
    return -(-rows // step) * step


def first_rows(count, height, bits):
    own, cross = shares(count)[0]
    return padded((len(own) + len(cross)) * UNIT + count * height, bits)


def second_rows(count, bits):
    return padded((len(own_blocks(count)) + count * (count // 2)) * UNIT, bits)


def smem_spec():
    return pl.BlockSpec(memory_space=pltpu.SMEM)


def vmem_spec():
    return pl.BlockSpec(memory_space=pltpu.VMEM)


def params(mebibytes):
    return pltpu.CompilerParams(vmem_limit_bytes=mebibytes * MIB)


def first_bit(orders, day, cell):
    return jnp.where(day == 0, (cell >> orders[0][0]) & 1, (cell >> orders[1][0]) & 1)


def own_gram_kernel(place, cell_map, pred, cell, start, first, second, panel):
    group = place[1]
    number = cell_map.shape[0]
    height = panel.shape[0]
    for t in range(number):
        slot = pl.multiple_of(lax.rem(cell_map[t], number) * LANES, LANES)
        panel[:, t * LANES : (t + 1) * LANES] = start[:, pl.ds(slot, LANES)]
    count = cell.shape[0] // UNIT
    row = 0
    scores = lax.dot_general(panel[...], cell[...], NT, preferred_element_type=F32)
    for c in range(count):
        first[row : row + height, :] = scores[:, c * LANES : (c + 1) * LANES]
        row += height
    for (i0, j0), (i1, j1) in zip(shares(count)[0][0], shares(count)[1][0]):
        left = rows_at(pred, i0 + group * (i1 - i0))
        right = rows_at(pred, j0 + group * (j1 - j0))
        first[row : row + UNIT, :] = lax.dot_general(left, right, NT, preferred_element_type=F32)
        row += UNIT
    row = 0
    for i in range(0, count, 2):
        right = cell[i * UNIT :, :]
        value = lax.dot_general(right[: 2 * UNIT, :], right, NT, preferred_element_type=F32)
        for r in range(2):
            for c in range(r, count - i):
                second[row : row + UNIT, :] = value[r * UNIT : (r + 1) * UNIT, c * UNIT : (c + 1) * UNIT]
                row += UNIT


def rows_at(whole, block):
    return whole[pl.ds(pl.multiple_of(block * UNIT, UNIT), UNIT), :]


def own_gram(place, cell_map, pred_own, cell_own, start):
    rows, width = pred_own.shape
    height = start.shape[0]
    count = rows // UNIT
    number = len(own_blocks(count))
    first = number // 2 * UNIT + count * height
    second = number * UNIT
    return pl.pallas_call(
        own_gram_kernel,
        out_shape=(jax.ShapeDtypeStruct((first, LANES), F32), jax.ShapeDtypeStruct((second, LANES), F32)),
        in_specs=[smem_spec()] * 2 + [vmem_spec()] * 3,
        out_specs=(vmem_spec(), vmem_spec()),
        scratch_shapes=[pltpu.VMEM((height, width), BF16)],
        compiler_params=params(16),
        name="own_gram",
    )(place, cell_map, pred_own, cell_own, start)


def own_tiles(tile_map, own, recv, whole, day):
    number = tile_map.shape[0]
    half = number // 2
    rows = own.shape[0]
    mine = pl.ds(pl.multiple_of(day * rows, rows), rows)
    theirs = pl.ds(pl.multiple_of((1 - day) * rows, rows), rows)
    for t in range(number):
        slot = lax.rem(tile_map[t], number)
        to = pl.ds(pl.multiple_of(lax.rem(slot, half) * LANES, LANES), LANES)

        @pl.when(lax.div(slot, half) == day)
        def _():
            whole[mine, to] = own[:, t * LANES : (t + 1) * LANES]
            whole[theirs, to] = recv[:, t * LANES : (t + 1) * LANES]


def cross_blocks(orders, shared, place, own, recv, part, home, away, left, right, scr):
    day, group, index = place[0], place[1], place[2]
    height, side = left.shape[0], right.shape[0]
    at_left = pl.ds(pl.multiple_of(group * height, height), height) if shared else pl.ds(0, height)
    at_right = pl.ds(pl.multiple_of(day * side, side), side)

    @pl.when(day == 0)
    def _():
        left[...] = own[at_left, :]
        right[...] = recv[at_right, :]

    @pl.when(day == 1)
    def _():
        left[...] = recv[at_left, :]
        right[...] = own[at_right, :]

    row = part.shape[0]
    scr[:row, :] = part[...]
    value = lax.dot_general(left[...], right[...], NT, preferred_element_type=F32)
    for i in range(height // UNIT):
        for j in range(side // UNIT):
            scr[row : row + UNIT, :] = value[i * UNIT : (i + 1) * UNIT, j * UNIT : (j + 1) * UNIT]
            row += UNIT
    if row < scr.shape[0]:
        scr[row:, :] = jnp.zeros((scr.shape[0] - row, LANES), F32)
    bit = first_bit(orders, day, index)
    rows = home.shape[0]
    home[...] = scr[pl.ds(pl.multiple_of(bit * rows, SUB), rows), :]
    away[...] = scr[pl.ds(pl.multiple_of((1 - bit) * rows, SUB), rows), :]


def first_cross_kernel(orders, place, own, recv, part, home, away, left, right, scr):
    cross_blocks(orders, True, place, own, recv, part, home, away, left, right, scr)


def second_cross_kernel(orders, place, pred_map, cell_map, pred_own, pred_recv, cell_own, cell_recv, part,
                        home, away, pred_tiles, cell_tiles, left, right, scr):
    cross_blocks(orders, False, place, cell_own, cell_recv, part, home, away, left, right, scr)
    own_tiles(pred_map, pred_own, pred_recv, pred_tiles, place[0])
    own_tiles(cell_map, cell_own, cell_recv, cell_tiles, place[0])


def first_cross(orders, total, place, own, recv, part):
    rows, width = own.shape
    out = jax.ShapeDtypeStruct((total // 2, LANES), F32)
    side = pltpu.VMEM((rows // 2, width), BF16)
    return pl.pallas_call(
        functools.partial(first_cross_kernel, orders),
        out_shape=(out, out),
        in_specs=[smem_spec()] + [vmem_spec()] * 3,
        out_specs=(vmem_spec(),) * 2,
        scratch_shapes=[side, side, pltpu.VMEM((total, LANES), F32)],
        compiler_params=params(12),
        name="first_cross",
    )(place, own, recv, part)


def second_cross(orders, total, place, pred_map, cell_map, pred_own, pred_recv, cell_own, cell_recv, part):
    rows, width = cell_own.shape
    out = jax.ShapeDtypeStruct((total // 2, LANES), F32)
    tiles = jax.ShapeDtypeStruct((2 * rows, width // 2), BF16)
    return pl.pallas_call(
        functools.partial(second_cross_kernel, orders),
        out_shape=(out, out, tiles, tiles),
        in_specs=[smem_spec()] * 3 + [vmem_spec()] * 5,
        out_specs=(vmem_spec(),) * 4,
        scratch_shapes=[
            pltpu.VMEM((rows, width), BF16),
            pltpu.VMEM((rows // 2, width), BF16),
            pltpu.VMEM((total, LANES), F32),
        ],
        compiler_params=params(12),
        name="second_cross",
    )(place, pred_map, cell_map, pred_own, pred_recv, cell_own, cell_recv, part)


def after(value, gate):
    return lax.optimization_barrier((value, gate))[0]


def bit_orders(bits):
    plain = list(range(bits))
    swapped = plain[:]
    if bits > 2:
        swapped[0], swapped[1] = 1, 0
    return plain, swapped


def cell_exchange(value, orders, stage, cells):
    pairs = []
    for c in range(cells):
        for d in range(2):
            pairs.append((2 * c + d, 2 * (c ^ (1 << orders[d][stage])) + d))
    return lax.ppermute(value, ("cell", "day"), pairs)


def other_core(value):
    return lax.ppermute(value, "day", [(0, 1), (1, 0)])


def other_group(value):
    return lax.ppermute(value, "group", [(0, 1), (1, 0)])


def halve(orders, stage, mine, recv):
    bit = jnp.where(lax.axis_index("day") == 0, orders[0][stage], orders[1][stage])
    own = (lax.axis_index("cell") >> bit) & 1
    half = mine.shape[0] // 2
    away = lax.dynamic_slice_in_dim(mine, (1 - own) * half, half, 0)
    away = away + lax.dynamic_slice_in_dim(recv, (1 - own) * half, half, 0)
    home = lax.dynamic_slice_in_dim(mine, own * half, half, 0)
    home = home + lax.dynamic_slice_in_dim(recv, own * half, half, 0)
    return home, away


def sum_chunks(orders, bits, cells, first, second):
    home, away = first
    late_home, late_away = second
    last = bits - 1
    recv = cell_exchange(away, orders, 0, cells)
    home, away = halve(orders, 1, home, recv)
    late_away = after(late_away, away)
    recv = cell_exchange(away, orders, 1, cells)
    late = cell_exchange(late_away, orders, 0, cells)
    for stage in range(2, last):
        home, away = halve(orders, stage, home, recv)
        recv = cell_exchange(away, orders, stage, cells)
    part = home + recv
    middle = cell_exchange(part, orders, last, cells)
    late_home, late_away = halve(orders, 1, late_home, after(late, part))
    late = cell_exchange(late_away, orders, 1, cells)
    for stage in range(2, last):
        late_home, late_away = halve(orders, stage, late_home, late)
        late = cell_exchange(late_away, orders, stage, cells)
    part = part + after(middle, late_away)
    late_part = after(late_home + late, part)
    for stage in reversed(range(1, last)):
        part = jnp.concatenate([part, cell_exchange(part, orders, stage, cells)], axis=0)
    late_middle = cell_exchange(late_part, orders, last, cells)
    other = other_group(part)
    rest = after(cell_exchange(part, orders, 0, cells), late_part)
    other_rest = other_group(rest)
    late_part = late_part + after(after(late_middle, rest), other)
    for stage in reversed(range(1, last)):
        recv = cell_exchange(late_part, orders, stage, cells)
        late_part = jnp.concatenate([late_part, recv if stage > 1 else after(recv, other_rest)], axis=0)
    late_rest = cell_exchange(late_part, orders, 0, cells)
    return (part, rest), (other, other_rest), (late_part, late_rest)


def place_sums(sources, target, core, bits, orders, cell):
    pieces = 1 << (bits - 1)
    rows = target.shape[1] // pieces
    for p in range(pieces):
        to = 0
        for stage in range(bits - 1):
            digit = (p >> (bits - 2 - stage)) & 1
            own = jnp.where(core == 0, (cell >> orders[0][stage]) & 1, (cell >> orders[1][stage]) & 1)
            to = 2 * to + (own ^ digit)
        begin = pl.multiple_of(to * rows, SUB)
        at = p % (pieces // 2) * rows
        target[core, pl.ds(begin, rows), :] = sources[p // (pieces // 2)][at : at + rows, :]


def split3(value):
    first = value.astype(BF16)
    rest = value - first.astype(F32)
    second = rest.astype(BF16)
    third = (rest - second.astype(F32)).astype(BF16)
    return first, second, third


def assemble(value, i, j, gram):
    rows, cols = pl.ds(i * UNIT, UNIT), pl.ds(j * UNIT, UNIT)
    for s, piece in enumerate(split3(value)):
        gram[s, rows, cols] = piece
    if i != j:
        for s, piece in enumerate(split3(value.T)):
            gram[s, cols, rows] = piece


def assemble_list(packed, core, row, count, own, cross, gram):
    for i, j in own:
        assemble(packed[core, row : row + UNIT, :], core * count + i, core * count + j, gram)
        row += UNIT
    for i, j in cross:
        assemble(packed[core, row : row + UNIT, :], i, count + core * (count // 2) + j, gram)
        row += UNIT


def exact_dot(left, right):
    return jnp.dot(left, right, precision=lax.Precision.HIGHEST, preferred_element_type=F32)


def inverse_factor(moments):
    size = moments.shape[0]
    row_ids = lax.broadcasted_iota(jnp.int32, (size, size), 0)
    col_ids = lax.broadcasted_iota(jnp.int32, (size, size), 1)
    work = jnp.concatenate([(row_ids == col_ids).astype(F32), moments], axis=1)
    shape = (SUB, 2 * size)
    sub = lax.broadcasted_iota(jnp.int32, shape, 0)
    rows = [work[SUB * i : SUB * i + SUB, :] for i in range(size // SUB)]
    out = []
    for b in range(size // SUB):
        lane = size + SUB * b
        head = rows[b]
        cols = [jnp.broadcast_to(head[:, lane + c : lane + c + 1], shape) for c in range(SUB)]
        entry = [[jnp.broadcast_to(cols[c][r : r + 1, :], shape) for c in range(r + 1)] for r in range(SUB)]
        y = [jnp.broadcast_to(head[r : r + 1, :], shape) for r in range(SUB)]
        inverse = []
        factor = [[None] * SUB for _ in range(SUB)]
        for k in range(SUB):
            inverse.append(1.0 / entry[k][k])
            for i in range(k + 1, SUB):
                factor[i][k] = entry[i][k] * inverse[k]
                for j in range(k + 1, i + 1):
                    entry[i][j] = entry[i][j] - factor[i][k] * entry[j][k]
                y[i] = y[i] - factor[i][k] * y[k]
        p = [y[k] * inverse[k] for k in range(SUB)]
        for i in reversed(range(SUB)):
            for k in range(i):
                p[k] = p[k] - factor[i][k] * p[i]
        for i in range(b + 1, size // SUB):
            terms = [jnp.broadcast_to(rows[i][:, lane + k : lane + k + 1], shape) * p[k] for k in range(SUB)]
            while len(terms) > 1:
                terms = [terms[t] + terms[t + 1] for t in range(0, len(terms), 2)]
            rows[i] = rows[i] - terms[0]
        result, pivot = y[0], entry[0][0]
        for k in range(1, SUB):
            result = jnp.where(sub == k, y[k], result)
            pivot = jnp.where(sub == k, entry[k][k], pivot)
        out.append(result * (1.0 / jnp.sqrt(pivot)))
    return jnp.concatenate(out, axis=0)[:, :size]


def half_step(scores, gram, cells):
    value = jnp.dot(scores, gram[0], preferred_element_type=F32)
    for s in range(1, SPLITS):
        value = value + jnp.dot(scores, gram[s], preferred_element_type=F32)
    moments = sum(
        lax.dot_general(piece, scores, NT, preferred_element_type=F32) for piece in split3(value)
    )
    return inverse_factor(moments / cells), value


def next_scores(inverse, value):
    return exact_dot(inverse, value).astype(BF16)


def first_chain_kernel(bits, orders, counts, place, a0, a1, y0, y1, a0_twin, a1_twin, y0_twin, y1_twin,
                       gram, scores_out, loadings_out, alpha, other):
    day, group, index = place[0], place[1], place[2]
    place_sums((a0, a1), alpha, day, bits, orders, index)
    place_sums((a0_twin, a1_twin), alpha, 1 - day, bits, orders, index)
    place_sums((y0, y1), other, day, bits, orders, index)
    place_sums((y0_twin, y1_twin), other, 1 - day, bits, orders, index)
    days = gram.shape[1]
    count = days // UNIT // 2
    height = scores_out.shape[0]

    def assemble_all(packs):
        for packed, (own, cross) in zip(packs, shares(count)):
            for core in range(2):
                assemble_list(packed, core, count * height, count, own, cross, gram)

    @pl.when(group == 0)
    def _():
        assemble_all((alpha, other))

    @pl.when(group == 1)
    def _():
        assemble_all((other, alpha))

    tiles = [alpha[core, c * height : (c + 1) * height, :] for core in range(2) for c in range(count)]
    scores = jnp.concatenate(tiles, axis=1).astype(BF16)
    scores_out[...] = scores
    inverse, value = half_step(scores, gram, counts[0])
    loadings_out[...] = next_scores(inverse, value)


def first_chain(bits, orders, counts, days, height, place, sums):
    panel = jax.ShapeDtypeStruct((height, days), BF16)
    packed = pltpu.VMEM((2, 2 * sums[0].shape[0], LANES), F32)
    return pl.pallas_call(
        functools.partial(first_chain_kernel, bits, orders, counts),
        out_shape=(jax.ShapeDtypeStruct((SPLITS, days, days), BF16), panel, panel),
        in_specs=[smem_spec()] + [vmem_spec()] * 8,
        out_specs=(vmem_spec(),) * 3,
        scratch_shapes=[packed, packed],
        compiler_params=params(20),
        name="first_chain",
    )(place, *sums)


def second_chain_kernel(bits, orders, counts, place, b0, b1, b0_twin, b1_twin, pred_gram,
                        scores_in, loadings_in, pred, cell, pred_out, cell_out, beta, cell_gram):
    day, index = place[0], place[2]
    place_sums((b0, b1), beta, day, bits, orders, index)
    place_sums((b0_twin, b1_twin), beta, 1 - day, bits, orders, index)
    days = pred.shape[0]
    count = days // UNIT // 2
    own = own_blocks(count)
    cross = [(i, j) for i in range(count) for j in range(count // 2)]
    for core in range(2):
        assemble_list(beta, core, 0, count, own, cross, cell_gram)
    pred_scores, loadings = scores_in[...], loadings_in[...]
    pred_inverse = pred_value = None
    for iteration in range(ITERS):
        if iteration > 0 or ITERS == 1:
            pred_inverse, pred_value = half_step(pred_scores, pred_gram, counts[0])
            loadings = next_scores(pred_inverse, pred_value)
        cell_inverse, cell_value = half_step(loadings, cell_gram, counts[1])
        if iteration < ITERS - 1:
            pred_scores = next_scores(cell_inverse, cell_value)
    raw = jnp.dot(pred_scores, pred[...], preferred_element_type=F32)
    pred_out[...] = exact_dot(pred_inverse, raw)
    raw = jnp.dot(loadings, cell[...], preferred_element_type=F32)
    cell_out[...] = exact_dot(cell_inverse, raw)


def second_chain(bits, orders, counts, place, sums, gram, scores, loadings, pred, cell):
    height, days = scores.shape
    out = jax.ShapeDtypeStruct((height, pred.shape[1]), F32)
    return pl.pallas_call(
        functools.partial(second_chain_kernel, bits, orders, counts),
        out_shape=(out, out),
        in_specs=[smem_spec()] + [vmem_spec()] * 9,
        out_specs=(vmem_spec(), vmem_spec()),
        scratch_shapes=[
            pltpu.VMEM((2, 2 * sums[0].shape[0], LANES), F32),
            pltpu.VMEM((SPLITS, days, days), BF16),
        ],
        compiler_params=params(24),
        name="second_chain",
    )(place, *sums, gram, scores, loadings, pred, cell)


def local(predictors, predictand, pred_map, cell_map, start_panel):
    cells = lax.axis_size("cell")
    bits = cells.bit_length() - 1
    orders = bit_orders(bits)
    days = predictors.shape[0] * 2
    height = start_panel.shape[0]
    counts = (float(predictors.shape[1] * cells), float(predictand.shape[1] * cells))
    place = jnp.stack([lax.axis_index("day"), lax.axis_index("group"), lax.axis_index("cell")])
    place = place.astype(jnp.int32)

    pred_recv = other_core(predictors)
    cell_recv = other_core(predictand)
    count = predictors.shape[0] // UNIT
    first_part, second_part = own_gram(place, cell_map, predictors, predictand, start_panel)
    first = first_cross(orders, first_rows(count, height, bits), place, predictors, pred_recv, first_part)
    home, away, pred, cell = second_cross(
        orders, second_rows(count, bits), place, pred_map, cell_map,
        predictors, pred_recv, predictand, after(cell_recv, first[1]), second_part,
    )
    second = (home, away)
    mine, other, late = sum_chunks(orders, bits, cells, first, second)
    sums = mine + other
    gram, scores, loadings = first_chain(
        bits, orders, counts, days, height, place, sums + tuple(other_core(part) for part in sums)
    )
    late = (late[0], after(late[1], loadings))
    late = late + tuple(other_core(part) for part in late)
    return second_chain(bits, orders, counts, place, late, gram, scores, loadings, pred, cell)


def solution(mesh):
    in_specs = (
        P("day", "cell"),
        P("day", ("group", "cell")),
        P("cell"),
        P(("group", "cell")),
        P(None, ("group", "cell")),
    )
    out_specs = (P(None, ("group", "cell", "day")), P(None, ("group", "cell", "day")))
    return jax.shard_map(local, mesh=mesh, in_specs=in_specs, out_specs=out_specs, check_vma=False)
```

```python
import functools

import jax
import jax.numpy as jnp
from jax import lax
from jax.experimental import pallas as pl
from jax.experimental.pallas import tpu as pltpu
from jax.sharding import PartitionSpec as P

ITERS = 3
LANES = 128
UNIT = 128
SPLITS = 3
SUB = 8
F32 = jnp.float32
BF16 = jnp.bfloat16
NT = (((1,), (1,)), ((), ()))
MIB = 1024 * 1024


def own_blocks(count):
    return [(i, j) for i in range(count) for j in range(i, count)]


def shares(count):
    own = own_blocks(count)
    cross = [(i, j) for i in range(count) for j in range(count // 2)]
    return [
        (own[: len(own) // 2], cross[: len(cross) // 2]),
        (own[len(own) // 2 :], cross[len(cross) // 2 :]),
    ]


def padded(rows, bits):
    step = SUB << (bits - 1)
    return -(-rows // step) * step


def first_rows(count, height, bits):
    own, cross = shares(count)[0]
    return padded((len(own) + len(cross)) * UNIT + count * height, bits)


def second_rows(count, bits):
    return padded((len(own_blocks(count)) + count * (count // 2)) * UNIT, bits)


def smem_spec():
    return pl.BlockSpec(memory_space=pltpu.SMEM)


def hbm_spec():
    return pl.BlockSpec(memory_space=pltpu.HBM)


def vmem_spec():
    return pl.BlockSpec(memory_space=pltpu.VMEM)


def params(mebibytes):
    return pltpu.CompilerParams(vmem_limit_bytes=mebibytes * MIB)


def first_bit(orders, day, cell):
    return jnp.where(day == 0, (cell >> orders[0][0]) & 1, (cell >> orders[1][0]) & 1)


def own_part_kernel(place, cell_map, pred_own, cell_own, start, out, pred, cell, panel, sems, tile_sems):
    group = place[1]
    number = cell_map.shape[0]
    height = panel.shape[0]
    loads = [pltpu.make_async_copy(pred_own, pred, sems.at[0]), pltpu.make_async_copy(cell_own, cell, sems.at[1])]
    for t in range(number):
        slot = pl.multiple_of(lax.rem(cell_map[t], number) * LANES, LANES)
        loads.append(
            pltpu.make_async_copy(
                start.at[:, pl.ds(slot, LANES)], panel.at[:, pl.ds(t * LANES, LANES)], tile_sems.at[t]
            )
        )
    for copy in loads:
        copy.start()
    count = cell.shape[0] // UNIT
    loads[0].wait()
    row = count * height
    for (i0, j0), (i1, j1) in zip(shares(count)[0][0], shares(count)[1][0]):
        left = rows_at(pred, i0 + group * (i1 - i0))
        right = rows_at(pred, j0 + group * (j1 - j0))
        out[row : row + UNIT, :] = lax.dot_general(left, right, NT, preferred_element_type=F32)
        row += UNIT
    for copy in loads[1:]:
        copy.wait()
    row = 0
    scores = lax.dot_general(panel[...], cell[...], NT, preferred_element_type=F32)
    for c in range(count):
        out[row : row + height, :] = scores[:, c * LANES : (c + 1) * LANES]
        row += height


def rows_at(whole, block):
    return whole[pl.ds(pl.multiple_of(block * UNIT, UNIT), UNIT), :]


def own_part(place, cell_map, pred_own, cell_own, start):
    rows, width = pred_own.shape
    height = start.shape[0]
    count = rows // UNIT
    size = len(own_blocks(count)) // 2 * UNIT + count * height
    return pl.pallas_call(
        own_part_kernel,
        out_shape=jax.ShapeDtypeStruct((size, LANES), F32),
        in_specs=[smem_spec()] * 2 + [hbm_spec()] * 3,
        out_specs=vmem_spec(),
        scratch_shapes=[
            pltpu.VMEM((rows, width), BF16),
            pltpu.VMEM((rows, width), BF16),
            pltpu.VMEM((height, width), BF16),
            pltpu.SemaphoreType.DMA((2,)),
            pltpu.SemaphoreType.DMA((cell_map.shape[0],)),
        ],
        compiler_params=params(57),
        name="own_part",
    )(place, cell_map, pred_own, cell_own, start)


def give(orders, place, scr, home, away):
    bit = first_bit(orders, place[0], place[2])
    rows = home.shape[0]
    away[...] = scr[pl.ds(pl.multiple_of((1 - bit) * rows, SUB), rows), :]
    home[...] = scr[pl.ds(pl.multiple_of(bit * rows, SUB), rows), :]


def cross_blocks(place, own, recv, scr, row, at_left, at_right):
    def run(left, right):
        to = row
        value = lax.dot_general(left[at_left, :], right[at_right, :], NT, preferred_element_type=F32)
        for i in range(value.shape[0] // UNIT):
            for j in range(value.shape[1] // UNIT):
                scr[to : to + UNIT, :] = value[i * UNIT : (i + 1) * UNIT, j * UNIT : (j + 1) * UNIT]
                to += UNIT
        if to < scr.shape[0]:
            scr[to:, :] = jnp.zeros((scr.shape[0] - to, LANES), F32)

    @pl.when(place[0] == 0)
    def _():
        run(own, recv)

    @pl.when(place[0] == 1)
    def _():
        run(recv, own)


def first_cross_kernel(orders, place, own, recv, part, home, away, scr):
    side = own.shape[0] // 2
    row = part.shape[0]
    scr[:row, :] = part[...]
    at_left = pl.ds(pl.multiple_of(place[1] * side, side), side)
    at_right = pl.ds(pl.multiple_of(place[0] * side, side), side)
    cross_blocks(place, own, recv, scr, row, at_left, at_right)
    give(orders, place, scr, home, away)


def second_cross_kernel(orders, place, own, recv, home, away, scr):
    count = own.shape[0] // UNIT
    row = 0
    for i in range(0, count, 2):
        right = own[i * UNIT :, :]
        value = lax.dot_general(right[: 2 * UNIT, :], right, NT, preferred_element_type=F32)
        for r in range(2):
            for c in range(r, count - i):
                scr[row : row + UNIT, :] = value[r * UNIT : (r + 1) * UNIT, c * UNIT : (c + 1) * UNIT]
                row += UNIT
    side = own.shape[0] // 2
    at_right = pl.ds(pl.multiple_of(place[0] * side, side), side)
    cross_blocks(place, own, recv, scr, row, pl.ds(0, own.shape[0]), at_right)
    give(orders, place, scr, home, away)


def cross(kernel, orders, total, name, place, own, recv, *part):
    out = jax.ShapeDtypeStruct((total // 2, LANES), F32)
    return pl.pallas_call(
        functools.partial(kernel, orders),
        out_shape=(out, out),
        in_specs=[smem_spec()] + [vmem_spec()] * (2 + len(part)),
        out_specs=(vmem_spec(),) * 2,
        scratch_shapes=[pltpu.VMEM((total, LANES), F32)],
        compiler_params=params(12),
        name=name,
    )(place, own, recv, *part)


def tiles_kernel(place, pred_map, cell_map, pred, pred_recv, cell, cell_recv, *outs):
    number = pred_map.shape[0]
    half = number // 2
    sources = ((pred_map, pred), (pred_map, pred_recv), (cell_map, cell), (cell_map, cell_recv))
    for (tile_map, stored), out in zip(sources, outs):
        for t in range(number):
            slot = lax.rem(tile_map[t], number)
            to = pl.ds(pl.multiple_of(lax.rem(slot, half) * LANES, LANES), LANES)

            @pl.when(lax.div(slot, half) == place[0])
            def _():
                out[:, to] = stored[:, t * LANES : (t + 1) * LANES]


def own_tiles(place, pred_map, cell_map, *fields):
    rows, width = fields[0].shape
    half = jax.ShapeDtypeStruct((rows, width // 2), BF16)
    return pl.pallas_call(
        tiles_kernel,
        out_shape=(half,) * 4,
        in_specs=[smem_spec()] * 3 + [vmem_spec()] * 4,
        out_specs=(vmem_spec(),) * 4,
        compiler_params=params(8),
        name="own_tiles",
    )(place, pred_map, cell_map, *fields)


def after(value, gate):
    return lax.optimization_barrier((value, gate))[0]


def bit_orders(bits):
    plain = list(range(bits))
    swapped = plain[:]
    if bits > 2:
        swapped[0], swapped[1] = 1, 0
    return plain, swapped


def cell_exchange(value, orders, stage, cells):
    pairs = []
    for c in range(cells):
        for d in range(2):
            pairs.append((2 * c + d, 2 * (c ^ (1 << orders[d][stage])) + d))
    return lax.ppermute(value, ("cell", "day"), pairs)


def other_core(value):
    return lax.ppermute(value, "day", [(0, 1), (1, 0)])


def other_group(value):
    return lax.ppermute(value, "group", [(0, 1), (1, 0)])


def halve(orders, stage, mine, recv):
    bit = jnp.where(lax.axis_index("day") == 0, orders[0][stage], orders[1][stage])
    own = (lax.axis_index("cell") >> bit) & 1
    half = mine.shape[0] // 2
    away = lax.dynamic_slice_in_dim(mine, (1 - own) * half, half, 0)
    away = away + lax.dynamic_slice_in_dim(recv, (1 - own) * half, half, 0)
    home = lax.dynamic_slice_in_dim(mine, own * half, half, 0)
    home = home + lax.dynamic_slice_in_dim(recv, own * half, half, 0)
    return home, away


def sum_chunks(orders, bits, cells, first, second):
    home, away = first
    late_home, late_away = second
    last = bits - 1
    recv = cell_exchange(away, orders, 0, cells)
    home, away = halve(orders, 1, home, recv)
    late_away = after(late_away, away)
    recv = cell_exchange(away, orders, 1, cells)
    late = cell_exchange(late_away, orders, 0, cells)
    for stage in range(2, last):
        home, away = halve(orders, stage, home, recv)
        recv = cell_exchange(away, orders, stage, cells)
    part = home + recv
    middle = cell_exchange(part, orders, last, cells)
    late_home, late_away = halve(orders, 1, late_home, after(late, part))
    late = cell_exchange(late_away, orders, 1, cells)
    for stage in range(2, last):
        late_home, late_away = halve(orders, stage, late_home, late)
        late = cell_exchange(late_away, orders, stage, cells)
    late_part = late_home + late
    part = part + after(middle, late_part)
    late_part = after(late_part, part)
    for stage in reversed(range(1, last)):
        part = jnp.concatenate([part, cell_exchange(part, orders, stage, cells)], axis=0)
    late_middle = cell_exchange(late_part, orders, last, cells)
    other = other_group(part)
    rest = after(cell_exchange(part, orders, 0, cells), late_part)
    other_rest = other_group(rest)
    late_part = late_part + after(after(late_middle, rest), other)
    for stage in reversed(range(1, last)):
        recv = cell_exchange(late_part, orders, stage, cells)
        late_part = jnp.concatenate([late_part, recv if stage > 1 else after(recv, other_rest)], axis=0)
    late_rest = cell_exchange(late_part, orders, 0, cells)
    return (part, rest), (other, other_rest), (late_part, late_rest)


def place_sums(sources, target, core, bits, orders, cell):
    pieces = 1 << (bits - 1)
    rows = target.shape[1] // pieces
    for p in range(pieces):
        to = 0
        for stage in range(bits - 1):
            digit = (p >> (bits - 2 - stage)) & 1
            own = jnp.where(core == 0, (cell >> orders[0][stage]) & 1, (cell >> orders[1][stage]) & 1)
            to = 2 * to + (own ^ digit)
        begin = pl.multiple_of(to * rows, SUB)
        at = p % (pieces // 2) * rows
        target[core, pl.ds(begin, rows), :] = sources[p // (pieces // 2)][at : at + rows, :]


def split3(value):
    first = value.astype(BF16)
    rest = value - first.astype(F32)
    second = rest.astype(BF16)
    third = (rest - second.astype(F32)).astype(BF16)
    return first, second, third


def assemble(value, i, j, gram):
    rows, cols = pl.ds(i * UNIT, UNIT), pl.ds(j * UNIT, UNIT)
    for s, piece in enumerate(split3(value)):
        gram[s, rows, cols] = piece
    if i != j:
        for s, piece in enumerate(split3(value.T)):
            gram[s, cols, rows] = piece


def assemble_list(packed, core, row, count, own, cross, gram):
    for i, j in own:
        assemble(packed[core, row : row + UNIT, :], core * count + i, core * count + j, gram)
        row += UNIT
    for i, j in cross:
        assemble(packed[core, row : row + UNIT, :], i, count + core * (count // 2) + j, gram)
        row += UNIT


def exact_dot(left, right):
    return jnp.dot(left, right, precision=lax.Precision.HIGHEST, preferred_element_type=F32)


def inverse_factor(moments):
    size = moments.shape[0]
    row_ids = lax.broadcasted_iota(jnp.int32, (size, size), 0)
    col_ids = lax.broadcasted_iota(jnp.int32, (size, size), 1)
    work = jnp.concatenate([(row_ids == col_ids).astype(F32), moments], axis=1)
    shape = (SUB, 2 * size)
    sub = lax.broadcasted_iota(jnp.int32, shape, 0)
    rows = [work[SUB * i : SUB * i + SUB, :] for i in range(size // SUB)]
    out = []
    for b in range(size // SUB):
        lane = size + SUB * b
        head = rows[b]
        cols = [jnp.broadcast_to(head[:, lane + c : lane + c + 1], shape) for c in range(SUB)]
        entry = [[jnp.broadcast_to(cols[c][r : r + 1, :], shape) for c in range(r + 1)] for r in range(SUB)]
        y = [jnp.broadcast_to(head[r : r + 1, :], shape) for r in range(SUB)]
        inverse = []
        factor = [[None] * SUB for _ in range(SUB)]
        for k in range(SUB):
            inverse.append(1.0 / entry[k][k])
            for i in range(k + 1, SUB):
                factor[i][k] = entry[i][k] * inverse[k]
                for j in range(k + 1, i + 1):
                    entry[i][j] = entry[i][j] - factor[i][k] * entry[j][k]
                y[i] = y[i] - factor[i][k] * y[k]
        p = [y[k] * inverse[k] for k in range(SUB)]
        for i in reversed(range(SUB)):
            for k in range(i):
                p[k] = p[k] - factor[i][k] * p[i]
        for i in range(b + 1, size // SUB):
            terms = [jnp.broadcast_to(rows[i][:, lane + k : lane + k + 1], shape) * p[k] for k in range(SUB)]
            while len(terms) > 1:
                terms = [terms[t] + terms[t + 1] for t in range(0, len(terms), 2)]
            rows[i] = rows[i] - terms[0]
        result, pivot = y[0], entry[0][0]
        for k in range(1, SUB):
            result = jnp.where(sub == k, y[k], result)
            pivot = jnp.where(sub == k, entry[k][k], pivot)
        out.append(result * (1.0 / jnp.sqrt(pivot)))
    return jnp.concatenate(out, axis=0)[:, :size]


def half_step(scores, gram, cells):
    value = jnp.dot(scores, gram[0], preferred_element_type=F32)
    for s in range(1, SPLITS):
        value = value + jnp.dot(scores, gram[s], preferred_element_type=F32)
    moments = sum(
        lax.dot_general(piece, scores, NT, preferred_element_type=F32) for piece in split3(value)
    )
    return inverse_factor(moments / cells), value


def next_scores(inverse, value):
    return exact_dot(inverse, value).astype(BF16)


def first_chain_kernel(bits, orders, counts, place, a0, a1, y0, y1, a0_twin, a1_twin, y0_twin, y1_twin,
                       gram, scores_out, loadings_out, alpha, other):
    day, group, index = place[0], place[1], place[2]
    place_sums((a0, a1), alpha, day, bits, orders, index)
    place_sums((a0_twin, a1_twin), alpha, 1 - day, bits, orders, index)
    place_sums((y0, y1), other, day, bits, orders, index)
    place_sums((y0_twin, y1_twin), other, 1 - day, bits, orders, index)
    days = gram.shape[1]
    count = days // UNIT // 2
    height = scores_out.shape[0]

    def assemble_all(packs):
        for packed, (own, cross) in zip(packs, shares(count)):
            for core in range(2):
                assemble_list(packed, core, count * height, count, own, cross, gram)

    @pl.when(group == 0)
    def _():
        assemble_all((alpha, other))

    @pl.when(group == 1)
    def _():
        assemble_all((other, alpha))

    tiles = [alpha[core, c * height : (c + 1) * height, :] for core in range(2) for c in range(count)]
    scores = jnp.concatenate(tiles, axis=1).astype(BF16)
    scores_out[...] = scores
    inverse, value = half_step(scores, gram, counts[0])
    loadings_out[...] = next_scores(inverse, value)


def first_chain(bits, orders, counts, days, height, place, sums):
    panel = jax.ShapeDtypeStruct((height, days), BF16)
    packed = pltpu.VMEM((2, 2 * sums[0].shape[0], LANES), F32)
    return pl.pallas_call(
        functools.partial(first_chain_kernel, bits, orders, counts),
        out_shape=(jax.ShapeDtypeStruct((SPLITS, days, days), BF16), panel, panel),
        in_specs=[smem_spec()] + [vmem_spec()] * 8,
        out_specs=(vmem_spec(),) * 3,
        scratch_shapes=[packed, packed],
        compiler_params=params(20),
        name="first_chain",
    )(place, *sums)


def second_chain_kernel(bits, orders, counts, place, b0, b1, b0_twin, b1_twin, pred_gram,
                        scores_in, loadings_in, pred, pred_recv, cell, cell_recv, pred_out, cell_out,
                        beta, cell_gram):
    day, index = place[0], place[2]
    place_sums((b0, b1), beta, day, bits, orders, index)
    place_sums((b0_twin, b1_twin), beta, 1 - day, bits, orders, index)
    days = pred_gram.shape[1]
    count = days // UNIT // 2
    own = own_blocks(count)
    cross = [(i, j) for i in range(count) for j in range(count // 2)]
    for core in range(2):
        assemble_list(beta, core, 0, count, own, cross, cell_gram)
    pred_scores, loadings = scores_in[...], loadings_in[...]
    pred_inverse = pred_value = None
    for iteration in range(ITERS):
        if iteration > 0 or ITERS == 1:
            pred_inverse, pred_value = half_step(pred_scores, pred_gram, counts[0])
            loadings = next_scores(pred_inverse, pred_value)
        cell_inverse, cell_value = half_step(loadings, cell_gram, counts[1])
        if iteration < ITERS - 1:
            pred_scores = next_scores(cell_inverse, cell_value)
    pred_out[...] = exact_dot(pred_inverse, panel(pred_scores, pred, pred_recv, day))
    cell_out[...] = exact_dot(cell_inverse, panel(loadings, cell, cell_recv, day))


def panel(scores, own, recv, day):
    half = own.shape[0]
    first, second = scores[:, :half].astype(F32), scores[:, half:].astype(F32)
    mine = jnp.where(day == 0, first, second).astype(BF16)
    theirs = jnp.where(day == 0, second, first).astype(BF16)
    value = jnp.dot(mine, own[...], preferred_element_type=F32)
    return value + jnp.dot(theirs, recv[...], preferred_element_type=F32)


def second_chain(bits, orders, counts, place, sums, gram, scores, loadings, tiles):
    height, days = scores.shape
    out = jax.ShapeDtypeStruct((height, tiles[0].shape[1]), F32)
    return pl.pallas_call(
        functools.partial(second_chain_kernel, bits, orders, counts),
        out_shape=(out, out),
        in_specs=[smem_spec()] + [vmem_spec()] * 11,
        out_specs=(vmem_spec(), vmem_spec()),
        scratch_shapes=[
            pltpu.VMEM((2, 2 * sums[0].shape[0], LANES), F32),
            pltpu.VMEM((SPLITS, days, days), BF16),
        ],
        compiler_params=params(24),
        name="second_chain",
    )(place, *sums, gram, scores, loadings, *tiles)


def local(predictors, predictand, pred_map, cell_map, start_panel):
    cells = lax.axis_size("cell")
    bits = cells.bit_length() - 1
    orders = bit_orders(bits)
    days = predictors.shape[0] * 2
    height = start_panel.shape[0]
    counts = (float(predictors.shape[1] * cells), float(predictand.shape[1] * cells))
    place = jnp.stack([lax.axis_index("day"), lax.axis_index("group"), lax.axis_index("cell")])
    place = place.astype(jnp.int32)

    pred_recv = other_core(predictors)
    cell_recv = other_core(predictand)
    count = predictors.shape[0] // UNIT
    part = own_part(place, cell_map, predictors, predictand, start_panel)
    first = cross(
        first_cross_kernel, orders, first_rows(count, height, bits), "first_cross", place, predictors, pred_recv, part
    )
    second = cross(
        second_cross_kernel, orders, second_rows(count, bits), "second_cross",
        place, predictand, after(cell_recv, first[1]),
    )

    mine, other, late = sum_chunks(orders, bits, cells, first, second)
    pred_again = other_core(after(predictors, mine[0]))
    cell_again = other_core(after(predictand, mine[0]))
    tiles = own_tiles(place, pred_map, cell_map, predictors, pred_again, predictand, cell_again)
    sums = mine + other
    gram, scores, loadings = first_chain(
        bits, orders, counts, days, height, place, sums + tuple(other_core(part) for part in sums)
    )
    late = (late[0], after(late[1], loadings))
    late = late + tuple(other_core(part) for part in late)
    return second_chain(bits, orders, counts, place, late, gram, scores, loadings, tiles)


def solution(mesh):
    in_specs = (
        P("day", "cell"),
        P("day", ("group", "cell")),
        P("cell"),
        P(("group", "cell")),
        P(None, ("group", "cell")),
    )
    out_specs = (P(None, ("group", "cell", "day")), P(None, ("group", "cell", "day")))
    return jax.shard_map(local, mesh=mesh, in_specs=in_specs, out_specs=out_specs, check_vma=False)
```

```python
import functools

import jax
import jax.numpy as jnp
from jax import lax
from jax.experimental import pallas as pl
from jax.experimental.pallas import tpu as pltpu
from jax.sharding import PartitionSpec as P

ITERS = 3
LANES = 128
UNIT = 128
SPLITS = 3
SUB = 8
F32 = jnp.float32
BF16 = jnp.bfloat16
NT = (((1,), (1,)), ((), ()))
MIB = 1024 * 1024


def own_blocks(count):
    return [(i, j) for i in range(count) for j in range(i, count)]


def shares(count):
    own = own_blocks(count)
    cross = [(i, j) for i in range(count) for j in range(count // 2)]
    return [
        (own[: len(own) // 2], cross[: len(cross) // 2]),
        (own[len(own) // 2 :], cross[len(cross) // 2 :]),
    ]


def padded(rows, bits):
    step = SUB << (bits - 1)
    return -(-rows // step) * step


def first_rows(count, height, bits):
    own, cross = shares(count)[0]
    return padded((len(own) + len(cross)) * UNIT + count * height, bits)


def second_rows(count, bits):
    return padded((len(own_blocks(count)) + count * (count // 2)) * UNIT, bits)


def smem_spec():
    return pl.BlockSpec(memory_space=pltpu.SMEM)


def hbm_spec():
    return pl.BlockSpec(memory_space=pltpu.HBM)


def vmem_spec():
    return pl.BlockSpec(memory_space=pltpu.VMEM)


def params(mebibytes):
    return pltpu.CompilerParams(vmem_limit_bytes=mebibytes * MIB)


def first_bit(orders, day, cell):
    return jnp.where(day == 0, (cell >> orders[0][0]) & 1, (cell >> orders[1][0]) & 1)


def own_part_kernel(place, cell_map, pred_own, cell_own, start, out, pred, cell, panel, sems, tile_sems):
    group = place[1]
    number = cell_map.shape[0]
    height = panel.shape[0]
    loads = [pltpu.make_async_copy(pred_own, pred, sems.at[0]), pltpu.make_async_copy(cell_own, cell, sems.at[1])]
    for t in range(number):
        slot = pl.multiple_of(lax.rem(cell_map[t], number) * LANES, LANES)
        loads.append(
            pltpu.make_async_copy(
                start.at[:, pl.ds(slot, LANES)], panel.at[:, pl.ds(t * LANES, LANES)], tile_sems.at[t]
            )
        )
    for copy in loads:
        copy.start()
    count = cell.shape[0] // UNIT
    loads[0].wait()
    row = count * height
    for (i0, j0), (i1, j1) in zip(shares(count)[0][0], shares(count)[1][0]):
        left = rows_at(pred, i0 + group * (i1 - i0))
        right = rows_at(pred, j0 + group * (j1 - j0))
        out[row : row + UNIT, :] = lax.dot_general(left, right, NT, preferred_element_type=F32)
        row += UNIT
    for copy in loads[1:]:
        copy.wait()
    row = 0
    scores = lax.dot_general(panel[...], cell[...], NT, preferred_element_type=F32)
    for c in range(count):
        out[row : row + height, :] = scores[:, c * LANES : (c + 1) * LANES]
        row += height


def rows_at(whole, block):
    return whole[pl.ds(pl.multiple_of(block * UNIT, UNIT), UNIT), :]


def own_part(place, cell_map, pred_own, cell_own, start):
    rows, width = pred_own.shape
    height = start.shape[0]
    count = rows // UNIT
    size = len(own_blocks(count)) // 2 * UNIT + count * height
    return pl.pallas_call(
        own_part_kernel,
        out_shape=jax.ShapeDtypeStruct((size, LANES), F32),
        in_specs=[smem_spec()] * 2 + [hbm_spec()] * 3,
        out_specs=vmem_spec(),
        scratch_shapes=[
            pltpu.VMEM((rows, width), BF16),
            pltpu.VMEM((rows, width), BF16),
            pltpu.VMEM((height, width), BF16),
            pltpu.SemaphoreType.DMA((2,)),
            pltpu.SemaphoreType.DMA((cell_map.shape[0],)),
        ],
        compiler_params=params(57),
        name="own_part",
    )(place, cell_map, pred_own, cell_own, start)


def give(orders, place, scr, home, away):
    bit = first_bit(orders, place[0], place[2])
    rows = home.shape[0]
    away[...] = scr[pl.ds(pl.multiple_of((1 - bit) * rows, SUB), rows), :]
    home[...] = scr[pl.ds(pl.multiple_of(bit * rows, SUB), rows), :]


def cross_blocks(place, own, recv, scr, row, at_left, at_right):
    def run(left, right):
        to = row
        value = lax.dot_general(left[at_left, :], right[at_right, :], NT, preferred_element_type=F32)
        for i in range(value.shape[0] // UNIT):
            for j in range(value.shape[1] // UNIT):
                scr[to : to + UNIT, :] = value[i * UNIT : (i + 1) * UNIT, j * UNIT : (j + 1) * UNIT]
                to += UNIT
        if to < scr.shape[0]:
            scr[to:, :] = jnp.zeros((scr.shape[0] - to, LANES), F32)

    @pl.when(place[0] == 0)
    def _():
        run(own, recv)

    @pl.when(place[0] == 1)
    def _():
        run(recv, own)


def first_cross_kernel(orders, place, own, recv, part, home, away, scr):
    side = own.shape[0] // 2
    row = part.shape[0]
    scr[:row, :] = part[...]
    at_left = pl.ds(pl.multiple_of(place[1] * side, side), side)
    at_right = pl.ds(pl.multiple_of(place[0] * side, side), side)
    cross_blocks(place, own, recv, scr, row, at_left, at_right)
    give(orders, place, scr, home, away)


def second_cross_kernel(orders, place, own, recv, home, away, scr):
    count = own.shape[0] // UNIT
    row = 0
    for i in range(0, count, 2):
        right = own[i * UNIT :, :]
        value = lax.dot_general(right[: 2 * UNIT, :], right, NT, preferred_element_type=F32)
        for r in range(2):
            for c in range(r, count - i):
                scr[row : row + UNIT, :] = value[r * UNIT : (r + 1) * UNIT, c * UNIT : (c + 1) * UNIT]
                row += UNIT
    side = own.shape[0] // 2
    at_right = pl.ds(pl.multiple_of(place[0] * side, side), side)
    cross_blocks(place, own, recv, scr, row, pl.ds(0, own.shape[0]), at_right)
    give(orders, place, scr, home, away)


def cross(kernel, orders, total, name, place, own, recv, *part):
    out = jax.ShapeDtypeStruct((total // 2, LANES), F32)
    return pl.pallas_call(
        functools.partial(kernel, orders),
        out_shape=(out, out),
        in_specs=[smem_spec()] + [vmem_spec()] * (2 + len(part)),
        out_specs=(vmem_spec(),) * 2,
        scratch_shapes=[pltpu.VMEM((total, LANES), F32)],
        compiler_params=params(12),
        name=name,
    )(place, own, recv, *part)


def tiles_kernel(place, pred_map, cell_map, pred, pred_recv, cell, cell_recv, *outs):
    number = pred_map.shape[0]
    half = number // 2
    outs = (outs[:2], outs[2:])
    for tile_map, own, recv, (mine, theirs) in ((pred_map, pred, pred_recv, outs[0]), (cell_map, cell, cell_recv, outs[1])):
        slots = [lax.rem(tile_map[t], number) for t in range(number)]
        for n in range(half):
            source = jnp.int32(0)
            for t in range(1, number):
                source = jnp.where(slots[t] == place[0] * half + n, t, source)
            at = pl.ds(pl.multiple_of(source * LANES, LANES), LANES)
            mine[:, n * LANES : (n + 1) * LANES] = own[:, at]
            theirs[:, n * LANES : (n + 1) * LANES] = recv[:, at]


def own_tiles(place, pred_map, cell_map, *fields):
    rows, width = fields[0].shape
    half = jax.ShapeDtypeStruct((rows, width // 2), BF16)
    return pl.pallas_call(
        tiles_kernel,
        out_shape=(half,) * 4,
        in_specs=[smem_spec()] * 3 + [vmem_spec()] * 4,
        out_specs=(vmem_spec(),) * 4,
        compiler_params=params(8),
        name="own_tiles",
    )(place, pred_map, cell_map, *fields)


def after(value, gate):
    return lax.optimization_barrier((value, gate))[0]


def bit_orders(bits):
    plain = list(range(bits))
    swapped = plain[:]
    if bits > 2:
        swapped[0], swapped[1] = 1, 0
    return plain, swapped


def cell_exchange(value, orders, stage, cells):
    pairs = []
    for c in range(cells):
        for d in range(2):
            pairs.append((2 * c + d, 2 * (c ^ (1 << orders[d][stage])) + d))
    return lax.ppermute(value, ("cell", "day"), pairs)


def other_core(value):
    return lax.ppermute(value, "day", [(0, 1), (1, 0)])


def other_group(value):
    return lax.ppermute(value, "group", [(0, 1), (1, 0)])


def halve(orders, stage, mine, recv):
    bit = jnp.where(lax.axis_index("day") == 0, orders[0][stage], orders[1][stage])
    own = (lax.axis_index("cell") >> bit) & 1
    half = mine.shape[0] // 2
    away = lax.dynamic_slice_in_dim(mine, (1 - own) * half, half, 0)
    away = away + lax.dynamic_slice_in_dim(recv, (1 - own) * half, half, 0)
    home = lax.dynamic_slice_in_dim(mine, own * half, half, 0)
    home = home + lax.dynamic_slice_in_dim(recv, own * half, half, 0)
    return home, away


def sum_chunks(orders, bits, cells, first, second):
    home, away = first
    late_home, late_away = second
    last = bits - 1
    recv = cell_exchange(away, orders, 0, cells)
    home, away = halve(orders, 1, home, recv)
    late_away = after(late_away, away)
    recv = cell_exchange(away, orders, 1, cells)
    late = cell_exchange(late_away, orders, 0, cells)
    for stage in range(2, last):
        home, away = halve(orders, stage, home, recv)
        recv = cell_exchange(away, orders, stage, cells)
    part = home + recv
    middle = cell_exchange(part, orders, last, cells)
    late_home, late_away = halve(orders, 1, late_home, after(late, part))
    late = cell_exchange(late_away, orders, 1, cells)
    for stage in range(2, last):
        late_home, late_away = halve(orders, stage, late_home, late)
        late = cell_exchange(late_away, orders, stage, cells)
    late_part = late_home + late
    part = part + after(middle, late_part)
    late_part = after(late_part, part)
    for stage in reversed(range(1, last)):
        part = jnp.concatenate([part, cell_exchange(part, orders, stage, cells)], axis=0)
    late_middle = cell_exchange(late_part, orders, last, cells)
    other = other_group(part)
    rest = after(cell_exchange(part, orders, 0, cells), late_part)
    other_rest = other_group(rest)
    late_part = late_part + after(after(late_middle, rest), other)
    for stage in reversed(range(1, last)):
        recv = cell_exchange(late_part, orders, stage, cells)
        late_part = jnp.concatenate([late_part, recv if stage > 1 else after(recv, other_rest)], axis=0)
    late_rest = cell_exchange(late_part, orders, 0, cells)
    return (part, rest), (other, other_rest), (late_part, late_rest)


def place_sums(sources, target, core, bits, orders, cell):
    pieces = 1 << (bits - 1)
    rows = target.shape[1] // pieces
    for p in range(pieces):
        to = 0
        for stage in range(bits - 1):
            digit = (p >> (bits - 2 - stage)) & 1
            own = jnp.where(core == 0, (cell >> orders[0][stage]) & 1, (cell >> orders[1][stage]) & 1)
            to = 2 * to + (own ^ digit)
        begin = pl.multiple_of(to * rows, SUB)
        at = p % (pieces // 2) * rows
        target[core, pl.ds(begin, rows), :] = sources[p // (pieces // 2)][at : at + rows, :]


def split3(value):
    first = value.astype(BF16)
    rest = value - first.astype(F32)
    second = rest.astype(BF16)
    third = (rest - second.astype(F32)).astype(BF16)
    return first, second, third


def assemble(value, i, j, gram):
    rows, cols = pl.ds(i * UNIT, UNIT), pl.ds(j * UNIT, UNIT)
    for s, piece in enumerate(split3(value)):
        gram[s, rows, cols] = piece
    if i != j:
        for s, piece in enumerate(split3(value.T)):
            gram[s, cols, rows] = piece


def assemble_list(packed, core, row, count, own, cross, gram):
    for i, j in own:
        assemble(packed[core, row : row + UNIT, :], core * count + i, core * count + j, gram)
        row += UNIT
    for i, j in cross:
        assemble(packed[core, row : row + UNIT, :], i, count + core * (count // 2) + j, gram)
        row += UNIT


def exact_dot(left, right):
    return jnp.dot(left, right, precision=lax.Precision.HIGHEST, preferred_element_type=F32)


def inverse_factor(moments):
    size = moments.shape[0]
    row_ids = lax.broadcasted_iota(jnp.int32, (size, size), 0)
    col_ids = lax.broadcasted_iota(jnp.int32, (size, size), 1)
    work = jnp.concatenate([(row_ids == col_ids).astype(F32), moments], axis=1)
    shape = (SUB, 2 * size)
    sub = lax.broadcasted_iota(jnp.int32, shape, 0)
    rows = [work[SUB * i : SUB * i + SUB, :] for i in range(size // SUB)]
    out = []
    while rows:
        lane = size + SUB * len(out)
        head, rows = rows[0], rows[1:]
        column = [[jnp.broadcast_to(r[:, lane + k : lane + k + 1], shape) for k in range(SUB)] for r in [head] + rows]
        top, column = column[0], column[1:]
        entry = [[jnp.broadcast_to(top[c][r : r + 1, :], shape) for c in range(r + 1)] for r in range(SUB)]
        y = [jnp.broadcast_to(head[r : r + 1, :], shape) for r in range(SUB)]
        for k in range(SUB):
            inverse = 1.0 / entry[k][k]
            scaled = y[k] * inverse
            factor = [entry[i][k] * inverse if i > k else None for i in range(SUB)]
            for i in range(k + 1, SUB):
                for j in range(k + 1, i + 1):
                    entry[i][j] = entry[i][j] - factor[i] * entry[j][k]
                y[i] = y[i] - factor[i] * y[k]
            for g in range(len(rows)):
                rows[g] = rows[g] - column[g][k] * scaled
                for i in range(k + 1, SUB):
                    column[g][i] = column[g][i] - factor[i] * column[g][k]
        result, pivot = y[0], entry[0][0]
        for k in range(1, SUB):
            result = jnp.where(sub == k, y[k], result)
            pivot = jnp.where(sub == k, entry[k][k], pivot)
        out.append(result * (1.0 / jnp.sqrt(pivot)))
    return jnp.concatenate(out, axis=0)[:, :size]


def half_step(scores, gram, cells):
    value = jnp.dot(scores, gram[0], preferred_element_type=F32)
    for s in range(1, SPLITS):
        value = value + jnp.dot(scores, gram[s], preferred_element_type=F32)
    moments = sum(
        lax.dot_general(piece, scores, NT, preferred_element_type=F32) for piece in split3(value)
    )
    return inverse_factor(moments / cells), value


def next_scores(inverse, value):
    return exact_dot(inverse, value).astype(BF16)


def first_chain_kernel(bits, orders, counts, place, a0, a1, y0, y1, a0_twin, a1_twin, y0_twin, y1_twin,
                       gram, scores_out, loadings_out, alpha, other):
    day, group, index = place[0], place[1], place[2]
    place_sums((a0, a1), alpha, day, bits, orders, index)
    place_sums((a0_twin, a1_twin), alpha, 1 - day, bits, orders, index)
    place_sums((y0, y1), other, day, bits, orders, index)
    place_sums((y0_twin, y1_twin), other, 1 - day, bits, orders, index)
    days = gram.shape[1]
    count = days // UNIT // 2
    height = scores_out.shape[0]

    def assemble_all(packs):
        for packed, (own, cross) in zip(packs, shares(count)):
            for core in range(2):
                assemble_list(packed, core, count * height, count, own, cross, gram)

    @pl.when(group == 0)
    def _():
        assemble_all((alpha, other))

    @pl.when(group == 1)
    def _():
        assemble_all((other, alpha))

    tiles = [alpha[core, c * height : (c + 1) * height, :] for core in range(2) for c in range(count)]
    scores = jnp.concatenate(tiles, axis=1).astype(BF16)
    scores_out[...] = scores
    inverse, value = half_step(scores, gram, counts[0])
    loadings_out[...] = next_scores(inverse, value)


def first_chain(bits, orders, counts, days, height, place, sums):
    panel = jax.ShapeDtypeStruct((height, days), BF16)
    packed = pltpu.VMEM((2, 2 * sums[0].shape[0], LANES), F32)
    return pl.pallas_call(
        functools.partial(first_chain_kernel, bits, orders, counts),
        out_shape=(jax.ShapeDtypeStruct((SPLITS, days, days), BF16), panel, panel),
        in_specs=[smem_spec()] + [vmem_spec()] * 8,
        out_specs=(vmem_spec(),) * 3,
        scratch_shapes=[packed, packed],
        compiler_params=params(20),
        name="first_chain",
    )(place, *sums)


def second_chain_kernel(bits, orders, counts, place, b0, b1, b0_twin, b1_twin, pred_gram,
                        scores_in, loadings_in, pred, pred_recv, cell, cell_recv, pred_out, cell_out,
                        beta, cell_gram):
    day, index = place[0], place[2]
    place_sums((b0, b1), beta, day, bits, orders, index)
    place_sums((b0_twin, b1_twin), beta, 1 - day, bits, orders, index)
    days = pred_gram.shape[1]
    count = days // UNIT // 2
    own = own_blocks(count)
    cross = [(i, j) for i in range(count) for j in range(count // 2)]
    for core in range(2):
        assemble_list(beta, core, 0, count, own, cross, cell_gram)
    pred_scores, loadings = scores_in[...], loadings_in[...]
    pred_inverse = pred_value = None
    for iteration in range(ITERS):
        if iteration > 0 or ITERS == 1:
            pred_inverse, pred_value = half_step(pred_scores, pred_gram, counts[0])
            loadings = next_scores(pred_inverse, pred_value)
        cell_inverse, cell_value = half_step(loadings, cell_gram, counts[1])
        if iteration < ITERS - 1:
            pred_scores = next_scores(cell_inverse, cell_value)
    pred_out[...] = exact_dot(pred_inverse, panel(pred_scores, pred, pred_recv, day))
    cell_out[...] = exact_dot(cell_inverse, panel(loadings, cell, cell_recv, day))


def panel(scores, own, recv, day):
    half = own.shape[0]
    first, second = scores[:, :half].astype(F32), scores[:, half:].astype(F32)
    mine = jnp.where(day == 0, first, second).astype(BF16)
    theirs = jnp.where(day == 0, second, first).astype(BF16)
    value = jnp.dot(mine, own[...], preferred_element_type=F32)
    return value + jnp.dot(theirs, recv[...], preferred_element_type=F32)


def second_chain(bits, orders, counts, place, sums, gram, scores, loadings, tiles):
    height, days = scores.shape
    out = jax.ShapeDtypeStruct((height, tiles[0].shape[1]), F32)
    return pl.pallas_call(
        functools.partial(second_chain_kernel, bits, orders, counts),
        out_shape=(out, out),
        in_specs=[smem_spec()] + [vmem_spec()] * 11,
        out_specs=(vmem_spec(), vmem_spec()),
        scratch_shapes=[
            pltpu.VMEM((2, 2 * sums[0].shape[0], LANES), F32),
            pltpu.VMEM((SPLITS, days, days), BF16),
        ],
        compiler_params=params(24),
        name="second_chain",
    )(place, *sums, gram, scores, loadings, *tiles)


def local(predictors, predictand, pred_map, cell_map, start_panel):
    cells = lax.axis_size("cell")
    bits = cells.bit_length() - 1
    orders = bit_orders(bits)
    days = predictors.shape[0] * 2
    height = start_panel.shape[0]
    counts = (float(predictors.shape[1] * cells), float(predictand.shape[1] * cells))
    place = jnp.stack([lax.axis_index("day"), lax.axis_index("group"), lax.axis_index("cell")])
    place = place.astype(jnp.int32)

    pred_recv = other_core(predictors)
    cell_recv = other_core(predictand)
    count = predictors.shape[0] // UNIT
    part = own_part(place, cell_map, predictors, predictand, start_panel)
    first = cross(
        first_cross_kernel, orders, first_rows(count, height, bits), "first_cross", place, predictors, pred_recv, part
    )
    second = cross(
        second_cross_kernel, orders, second_rows(count, bits), "second_cross",
        place, predictand, after(cell_recv, first[1]),
    )

    mine, other, late = sum_chunks(orders, bits, cells, first, second)
    pred_again = other_core(after(predictors, mine[0]))
    cell_again = other_core(after(predictand, mine[0]))
    tiles = own_tiles(place, pred_map, cell_map, predictors, pred_again, predictand, cell_again)
    sums = mine + other
    gram, scores, loadings = first_chain(
        bits, orders, counts, days, height, place, sums + tuple(other_core(part) for part in sums)
    )
    late = (late[0], after(late[1], loadings))
    late = late + tuple(other_core(part) for part in late)
    return second_chain(bits, orders, counts, place, late, gram, scores, loadings, tiles)


def solution(mesh):
    in_specs = (
        P("day", "cell"),
        P("day", ("group", "cell")),
        P("cell"),
        P(("group", "cell")),
        P(None, ("group", "cell")),
    )
    out_specs = (P(None, ("group", "cell", "day")), P(None, ("group", "cell", "day")))
    return jax.shard_map(local, mesh=mesh, in_specs=in_specs, out_specs=out_specs, check_vma=False)
```
